128 devices in a mesh: gx: 16 (over y, z), gy: 8 (over x, core).
Axes of the slice: x: 4, y: 4, z: 4, core: 2. Of those that a mesh axis runs over, the one named last changes fastest.
Arguments:
- u_now: float32 [3, 256, 256, 128], P(None, 'gx', 'gy'), may hold values from -3 to 3
- u_prev: float32 [3, 256, 256, 128], P(None, 'gx', 'gy'), may hold values from -3 to 3
- density: float32 [256, 256, 128], P('gx', 'gy'), may hold values from 1 to 2
- shear_mod: float32 [256, 256, 128], P('gx', 'gy'), may hold values from 0.4 to 1
- lame_first: float32 [256, 256, 128], P('gx', 'gy'), may hold values from 0.4 to 1
- storey_disp: float32 [3, 64, 131072], P(None, None, ('gx', 'gy')), may hold values from -2 to 2
- storey_vel: float32 [3, 64, 131072], P(None, None, ('gx', 'gy')), may hold values from -2 to 2
- hyst_fraction: float32 [3, 64, 131072], P(None, None, ('gx', 'gy')), may hold values from -1 to 1
- branch_flags: int32 [3, 64, 131072], P(None, None, ('gx', 'gy')), may hold values from 0 to 2
- stiffness: float32 [64, 131072], P(None, ('gx', 'gy')), may hold values from 0.5 to 2
- storey_mass: float32 [64, 131072], P(None, ('gx', 'gy')), may hold values from 0.7 to 1.4
- yield_drift: float32 [64, 131072], P(None, ('gx', 'gy')), may hold values from 0.1 to 1
- storey_count: int32 [131072], P(('gx', 'gy')), may hold values from 8 to 64
- footprint_tile: int32 [131072, 1], P(('gx', 'gy')), may hold values from 0 to 127; in each aligned block of 1024 rows (0 to 1023, 1024 to 2047, ...) at most 16 rows name the same one
- footprint_cell: int32 [131072], P(('gx', 'gy')), may hold values from 0 to 511
Outputs:
- field_now: float32 [3, 256, 256, 128], P(None, 'gx', 'gy')
- field_before: float32 [3, 256, 256, 128], P(None, 'gx', 'gy')
- final_disp: float32 [3, 64, 131072], P(None, None, ('gx', 'gy'))
- final_vel: float32 [3, 64, 131072], P(None, None, ('gx', 'gy'))
- final_hyst: float32 [3, 64, 131072], P(None, None, ('gx', 'gy'))
The draws below stay inside these ranges and needn't reach their ends.
Inputs may be any that keep to these rules, and one draw needn't show every extreme that they name: `footprint_tile`: among the buildings of one device at most 16 name the same tile, a bound that some block reaches.
All inputs are finite; a program needn't handle non-finite values.
Results may differ from the reference program's by a relative error of at most 0.000061.
Values sent between devices are 32-bit elements; how exact they have to be, the bound alone decides.
No kernel may reach another device: no remote copies, remote signals or barrier semaphores. Data moves between devices by JAX's collectives and lax.ppermute only.
A program may use at most 128 MiB of HBM per device.

```python
import math
import jax
import jax.numpy as jnp
import numpy as np

CX = 16
CY = 32
CZ = 128
BPD = 1024
STOREYS = 64
STEPS = 8
NX = 256
NY = 256
NB = 131072
CAP = 16
N_GY = 8
DEVICES = 128


def place_ends(entries, key, least, top_value):
    place = [jax.random.randint(jax.random.fold_in(key, axis), (), 0, length) for axis, length in enumerate(entries.shape)]
    widest = entries.shape.index(max(entries.shape))
    next_to = place[:widest] + [(place[widest] + 1) % entries.shape[widest]] + place[widest + 1:]
    return entries.at[tuple(place)].set(least).at[tuple(next_to)].set(top_value)


def block_scale(own_key, extent, cuts, smallest, top_value):
    gain, own = 1.0, jax.random.fold_in(own_key, 6)
    for axis_at, shards_of in cuts:
        draws = jnp.exp(jax.random.uniform(jax.random.fold_in(own, axis_at), (shards_of,), jnp.float32, smallest / len(cuts), top_value / len(cuts)))
        gain = gain * jnp.repeat(draws, extent[axis_at] // shards_of).reshape([-1 if axis == axis_at else 1 for axis in range(len(extent))])
    return gain


def deal_out(rng, own, number, rows, number_of, top, limit, lean):
    ranking = jax.random.permutation(rng, number_of)
    heavy_load, usual = shares(number_of, rows * top, limit, lean, True), shares(number_of, rows * top, limit, lean, False)
    places = jnp.arange(number_of)

    def named(tallies, offset_by):
        used = int((tallies > 0).sum())
        fixed = max(1, used // 4)
        moved = fixed + (places - fixed + offset_by * (used - fixed)) % max(1, number_of - fixed)
        return jnp.zeros((number_of,), jnp.int32).at[ranking[jnp.where(places < fixed, places, moved)]].set(jnp.asarray(tallies, jnp.int32))

    tallies = jnp.where(number % 4 == 0, named(heavy_load, number // 4), named(usual, number - number // 4 - 1))
    mixed = jax.random.permutation(jax.random.fold_in(own, 3), number_of)
    donor, taker = mixed[0:number_of // 2 * 2:2], mixed[1:number_of // 2 * 2:2]
    slack = jnp.minimum(tallies[donor] - 1, limit - tallies[taker]) // 2
    slack = jnp.where((donor == ranking[0]) | (taker == ranking[0]) | (tallies[taker] == 0), 0, jnp.maximum(slack, 0))
    moved = jax.random.randint(jax.random.fold_in(own, 4), (number_of // 2,), 0, 1 << 20) % (slack + 1)
    tallies = tallies.at[donor].add(-moved).at[taker].add(moved)
    members = jnp.searchsorted(jnp.cumsum(tallies), jnp.arange(rows * top), side="right").astype(jnp.int32)
    table = members.reshape(top, rows).T
    table = table[jax.random.permutation(jax.random.fold_in(own, 1), rows)]
    offset_by = jax.random.randint(jax.random.fold_in(own, 2), (rows, 1), 0, top)
    return jnp.take_along_axis(table, (jnp.arange(top)[None, :] + offset_by) % top, axis=1)


def shares(count, total, limit, lean, full):
    loads = [(1 << 20) // math.isqrt(standing ** lean) + 1 for standing in range(1, count + 1)]
    largest = limit if full else min(limit, max(-(-total // count), total * loads[0] // sum(loads)))
    least = 1 if total - largest >= count - 1 else 0
    counts, spare = [largest] + [least] * (count - 1), total - largest - least * (count - 1)
    while spare > 0:
        candidates = [i for i in range(1, count) if counts[i] < largest] or [i for i in range(1, count) if counts[i] < limit]
        mass, left = sum([loads[i] for i in candidates]), spare
        for i in candidates:
            extra = min(limit - counts[i], max(1, left * loads[i] // mass), spare)
            counts[i] = counts[i] + extra
            spare = spare - extra
    return np.array(counts)


def normal_values(rng, extent, width, limit, pieces=(), kind=jnp.bfloat16):
    gain = block_scale(rng, extent, pieces, -0.22, 0.18) if pieces else 1.0
    array = jax.random.normal(rng, extent, jnp.float32) * width * gain
    return jnp.minimum(jnp.maximum(array, -limit), limit).astype(kind)


def setup_inputs(seed: int = 0) -> dict:
    streams_of = jax.random.split(jax.random.key(seed), 16)
    u_now = normal_values(streams_of[0], (3, NX, NY, CZ), 0.5, 3.0, ((1, 16), (2, 8)), jnp.float32)
    u_prev = normal_values(streams_of[1], (3, NX, NY, CZ), 0.5, 3.0, ((1, 16), (2, 8)), jnp.float32)
    density = jnp.clip(jnp.exp(math.log(2.0) - 0.6931472 * jax.random.uniform(streams_of[2], (NX, NY, CZ), jnp.float32) ** block_scale(streams_of[2], (NX, NY, CZ), ((0, 16), (1, 8)), -0.2, 0.2)), 1.0, 2.0)
    shear_mod = jnp.clip(jnp.exp(math.log(1.0) - 0.9162907 * jax.random.uniform(streams_of[3], (NX, NY, CZ), jnp.float32) ** block_scale(streams_of[3], (NX, NY, CZ), ((0, 16), (1, 8)), -0.2, 0.2)), 0.4, 1.0)
    lame_first = jnp.clip(jnp.exp(math.log(1.0) - 0.9162907 * jax.random.uniform(streams_of[4], (NX, NY, CZ), jnp.float32) ** block_scale(streams_of[4], (NX, NY, CZ), ((0, 16), (1, 8)), -0.2, 0.2)), 0.4, 1.0)
    storey_disp = normal_values(streams_of[5], (3, STOREYS, NB), 0.3, 2.0, ((2, 128),), jnp.float32)
    storey_vel = normal_values(streams_of[6], (3, STOREYS, NB), 0.3, 2.0, ((2, 128),), jnp.float32)
    hyst_fraction = jnp.clip(jax.random.uniform(streams_of[7], (3, STOREYS, NB), jnp.float32, -1.0, 1.0) * block_scale(streams_of[7], (3, STOREYS, NB), ((2, 128),), -0.4, 0.0), -1.0, 1.0)
    branch_flags = place_ends(jax.random.randint(streams_of[8], (3, STOREYS, NB), 0, 3), jax.random.fold_in(streams_of[8], 1), 0, 2).astype(jnp.int32)
    stiffness = jnp.clip(jnp.exp(math.log(2.0) - 1.3862944 * jax.random.uniform(streams_of[9], (STOREYS, NB), jnp.float32) ** block_scale(streams_of[9], (STOREYS, NB), ((1, 128),), -0.2, 0.2)), 0.5, 2.0)
    storey_mass = jnp.clip(jnp.exp(math.log(1.4) - 0.6931472 * jax.random.uniform(streams_of[10], (STOREYS, NB), jnp.float32) ** block_scale(streams_of[10], (STOREYS, NB), ((1, 128),), -0.2, 0.2)), 0.7, 1.4)
    yield_drift = jnp.clip(jnp.exp(math.log(1.0) - 2.3025851 * jax.random.uniform(streams_of[11], (STOREYS, NB), jnp.float32) ** block_scale(streams_of[11], (STOREYS, NB), ((1, 128),), -0.2, 0.2)), 0.1, 1.0)
    storey_count = place_ends(jax.random.randint(streams_of[12], (NB,), 8, STOREYS + 1), jax.random.fold_in(streams_of[12], 1), 8, STOREYS).astype(jnp.int32)
    footprint_tile_keys = jax.random.split(jax.random.fold_in(streams_of[13], 1), NB // BPD)
    footprint_tile_turns = jax.random.permutation(jax.random.fold_in(streams_of[13], 3), NB // BPD)
    footprint_tile = jax.vmap(lambda own, number: deal_out(jax.random.fold_in(streams_of[13], 2), own, number, BPD, DEVICES, 1, CAP, 2))(footprint_tile_keys, footprint_tile_turns).reshape((NB, 1))
    footprint_cell = place_ends(jax.random.randint(streams_of[14], (NB,), 0, CX * CY), jax.random.fold_in(streams_of[14], 1), 0, (CX * CY) - 1).astype(jnp.int32)
    return dict(u_now=u_now, u_prev=u_prev, density=density, shear_mod=shear_mod, lame_first=lame_first, storey_disp=storey_disp, storey_vel=storey_vel, hyst_fraction=hyst_fraction, branch_flags=branch_flags, stiffness=stiffness, storey_mass=storey_mass, yield_drift=yield_drift, storey_count=storey_count, footprint_tile=footprint_tile, footprint_cell=footprint_cell)


time_step = 0.35
post_share = 0.1
damping_rate = 0.05


def shifted(padded, direction, offset):
    starts = [2, 2, 2]
    starts[direction] = starts[direction] + offset
    size_x = padded.shape[-3] - 4
    size_y = padded.shape[-2] - 4
    size_z = padded.shape[-1] - 4
    return padded[..., starts[0]:starts[0] + size_x, starts[1]:starts[1] + size_y, starts[2]:starts[2] + size_z]


def central(padded, direction):
    near = shifted(padded, direction, 1) - shifted(padded, direction, -1)
    far_part = shifted(padded, direction, 2) - shifted(padded, direction, -2)
    return (8.0 * near - far_part) / 12.0


def stresses(padded, lame, shear_value):
    gradients = [[central(padded[component], direction) for direction in range(3)] for component in range(3)]
    trace_sum = gradients[0][0] + gradients[1][1] + gradients[2][2]
    normal_x = lame * trace_sum + 2.0 * shear_value * gradients[0][0]
    normal_y = lame * trace_sum + 2.0 * shear_value * gradients[1][1]
    normal_z = lame * trace_sum + 2.0 * shear_value * gradients[2][2]
    shear_xy = shear_value * (gradients[0][1] + gradients[1][0])
    shear_xz = shear_value * (gradients[0][2] + gradients[2][0])
    shear_yz = shear_value * (gradients[1][2] + gradients[2][1])
    return jnp.stack([normal_x, normal_y, normal_z, shear_xy, shear_xz, shear_yz])


def divergence(padded):
    force_x = central(padded[0], 0) + central(padded[3], 1) + central(padded[4], 2)
    force_y = central(padded[3], 0) + central(padded[1], 1) + central(padded[5], 2)
    force_z = central(padded[4], 0) + central(padded[5], 1) + central(padded[2], 2)
    return jnp.stack([force_x, force_y, force_z])


def pad_grid(field):
    return jnp.pad(field, ((0, 0), (2, 2), (2, 2), (2, 2)))


def drifts(disp):
    lower = jnp.concatenate([jnp.zeros_like(disp[:, :1]), disp[:, :-1]], axis=1)
    return disp - lower


def building_start(storey_disp, storey_vel, hyst_fraction, branch_flags, yield_drift, storey_count):
    levels = storey_disp.shape[1]
    storey_mask = (jnp.arange(levels, dtype=jnp.int32)[:, None] < storey_count[None, :]).astype(jnp.float32)
    disp = storey_disp * storey_mask
    vel = storey_vel * storey_mask
    elastic = hyst_fraction * yield_drift
    hyst = jnp.where(branch_flags == 1, yield_drift, jnp.where(branch_flags == 2, -yield_drift, elastic)) * storey_mask
    return storey_mask, disp, vel, hyst, drifts(disp)


def building_step(disp, vel, hyst, drift, ground, stiffness, storey_mass, yield_drift, storey_mask):
    spring = stiffness * (post_share * drift + (1.0 - post_share) * hyst) * storey_mask
    above = jnp.concatenate([spring[:, 1:], jnp.zeros_like(spring[:, :1])], axis=1)
    accel = (above - spring) / storey_mass - damping_rate * vel - ground[:, None, :]
    vel = (vel + time_step * accel) * storey_mask
    disp = (disp + time_step * vel) * storey_mask
    new_drift = drifts(disp)
    hyst = jnp.clip(hyst + new_drift - drift, -yield_drift, yield_drift) * storey_mask
    return disp, vel, hyst, new_drift


def reference(u_now, u_prev, density, shear_mod, lame_first, storey_disp, storey_vel, hyst_fraction, branch_flags, stiffness, storey_mass, yield_drift, storey_count, footprint_tile, footprint_cell):
    current = u_now
    previous = u_prev
    surfaces = []
    for timestep in range(STEPS):
        stress = stresses(pad_grid(current), lame_first, shear_mod)
        accel = divergence(pad_grid(stress)) / density
        surfaces.append(accel[:, :, :, 0])
        current, previous = 2.0 * current - previous + time_step * time_step * accel, current
    history = jnp.stack(surfaces)
    owner_tile = footprint_tile[:, 0]
    rows_x = (owner_tile // N_GY) * CX + footprint_cell // CY
    rows_y = (owner_tile % N_GY) * CY + footprint_cell % CY
    ground = history[:, :, rows_x, rows_y]
    storey_mask, disp, vel, hyst, drift = building_start(storey_disp, storey_vel, hyst_fraction, branch_flags, yield_drift, storey_count)
    for timestep in range(STEPS):
        disp, vel, hyst, drift = building_step(disp, vel, hyst, drift, ground[timestep], stiffness, storey_mass, yield_drift, storey_mask)
    return current, previous, disp, vel, hyst
```

```python
import jax
import jax.numpy as jnp
from jax import lax
from jax.experimental import pallas as pl
from jax.experimental.pallas import tpu as pltpu
from jax.sharding import PartitionSpec as P

STEPS = 8
DT = 0.35
POST = 0.1
DAMP = 0.05
F32 = jnp.float32
BF16 = jnp.bfloat16
VM = pl.BlockSpec(memory_space=pltpu.VMEM)
SM = pl.BlockSpec(memory_space=pltpu.SMEM)
HB = pl.BlockSpec(memory_space=pl.ANY)
CP = pltpu.CompilerParams(vmem_limit_bytes=56 << 20)
YR = 56

XPARTS = ((0, 3, 8), (1, 3, 4), (2, 1, 6), (3, 1, 6), (4, 1, 4))
XPLANES = sum(c * w for _, c, w in XPARTS)
YBLOCKS = sum(c * (16 + 2 * w) for _, c, w in XPARTS)


def sds(*shape):
    return jax.ShapeDtypeStruct(shape, F32)


def ring(x, axis, step):
    n = lax.axis_size(axis)
    return lax.ppermute(x, axis, [(i, (i + step) % n) for i in range(n)])


def split3(x):
    hi = x.astype(BF16)
    rest = x - hi.astype(F32)
    mid = rest.astype(BF16)
    low = (rest - mid.astype(F32)).astype(BF16)
    return hi, mid, low


def at_comp(ref, comps, c, rows, cols):
    return ref.at[c, rows, cols] if comps == 3 else ref.at[rows, cols]


def pack_x_kernel(u, p, la, mu, de, up, down, sem):
    args = (u, p, la, mu, de)
    copies = []
    off = 0
    for a, comps, w in XPARTS:
        for c in range(comps):
            full = pl.ds(0, 32)
            src_up = at_comp(args[a], comps, c, pl.ds(16 - w, w), full)
            src_dn = at_comp(args[a], comps, c, pl.ds(0, w), full)
            n = len(copies)
            copies.append(pltpu.make_async_copy(src_up, up.at[pl.ds(off, w)], sem.at[n]))
            copies.append(pltpu.make_async_copy(src_dn, down.at[pl.ds(off, w)], sem.at[n + 1]))
            off += w
    for cp in copies:
        cp.start()
    for cp in copies:
        cp.wait()


def pack_y_kernel(u, p, la, mu, de, north, south, up, down, sem):
    args = (u, p, la, mu, de)
    copies = []
    off = 0
    src = 0
    for a, comps, w in XPARTS:
        for c in range(comps):
            for dst, col in ((up, 24), (down, 0)):
                n = len(copies)
                s = at_comp(args[a], comps, c, pl.ds(0, 16), pl.ds(col, 8))
                cp = pltpu.make_async_copy(s, dst.at[pl.ds(off + w, 16)], sem.at[n])
                cp.start()
                copies.append(cp)
                dst[off : off + w] = north[src : src + w, col : col + 8]
                dst[off + w + 16 : off + 2 * w + 16] = south[src : src + w, col : col + 8]
            off += 16 + 2 * w
            src += w
    for cp in copies:
        cp.wait()


def pack_round_kernel(top, bot, north, south, up, down):
    for dst, col in ((up, 24), (down, 0)):
        dst[:, 0:8] = north[:, :, col : col + 8]
        dst[:, 8:16] = top[:, :, col : col + 8]
        dst[:, 16:24] = bot[:, :, col : col + 8]
        dst[:, 24:32] = south[:, :, col : col + 8]


def lane_coefs():
    z = lax.broadcasted_iota(jnp.int32, (8, 128), 1)
    one = jnp.full((8, 128), 1.0, F32)
    zero = jnp.zeros((8, 128), F32)
    return (
        jnp.where(z < 127, 8.0 * one, zero),
        jnp.where(z >= 1, 8.0 * one, zero),
        jnp.where(z < 126, one, zero),
        jnp.where(z >= 2, one, zero),
    )


def dz(f, coefs):
    cp1, cm1, cp2, cm2 = coefs
    near = cp1 * pltpu.roll(f, 127, 1) - cm1 * pltpu.roll(f, 1, 1)
    far = cp2 * pltpu.roll(f, 126, 1) - cm2 * pltpu.roll(f, 2, 1)
    return near - far


def dx(ref, c, x, y):
    ys = pl.ds(y, 8)
    near = ref[c, x + 1, ys] - ref[c, x - 1, ys]
    far = ref[c, x + 2, ys] - ref[c, x - 2, ys]
    return 8.0 * near - far


def dy(ref, c, x, y):
    near = ref[c, x, pl.ds(y + 1, 8)] - ref[c, x, pl.ds(y - 1, 8)]
    far = ref[c, x, pl.ds(y + 2, 8)] - ref[c, x, pl.ds(y - 2, 8)]
    return 8.0 * near - far


def stress_pass(u, ux, s, lam, mu, x0, nx, y0, blocks):
    def body(i, carry):
        coefs = lane_coefs()
        gx = i + x0
        x = gx - ux
        for b in range(blocks):
            y = y0 + 8 * b
            ys = pl.ds(y, 8)
            m = mu[gx - 2, ys]
            la = lam[gx - 2, ys]
            g00 = dx(u, 0, x, y)
            g11 = dy(u, 1, x, y)
            g22 = dz(u[2, x, ys], coefs)
            lt = la * (g00 + g11 + g22)
            m2 = m + m
            s[0, gx, ys] = lt + m2 * g00
            s[1, gx, ys] = lt + m2 * g11
            s[2, gx, ys] = lt + m2 * g22
            s[3, gx, ys] = m * (dy(u, 0, x, y) + dx(u, 1, x, y))
            s[4, gx, ys] = m * (dz(u[0, x, ys], coefs) + dx(u, 2, x, y))
            s[5, gx, ys] = m * (dz(u[1, x, ys], coefs) + dy(u, 2, x, y))
        return carry

    lax.fori_loop(0, nx, body, 0)


def force(s, q, x, y, coefs):
    ys = pl.ds(y, 8)
    f0 = dx(s, 0, x, y) + dy(s, 3, x, y) + dz(s[4, x, ys], coefs)
    f1 = dx(s, 3, x, y) + dy(s, 1, x, y) + dz(s[5, x, ys], coefs)
    f2 = dx(s, 4, x, y) + dy(s, 5, x, y) + dz(s[2, x, ys], coefs)
    return q * f0, q * f1, q * f2


def surface(fs, slot, old):
    lane = lax.broadcasted_iota(jnp.int32, (8, 128), 1)
    for c, f in enumerate(fs):
        v = pltpu.roll(f, slot + c, 1) if slot + c else f
        old = jnp.where(lane == slot + c, v, old)
    return old


def wave_two_steps(ue, prev, lam, mu, q, s, hs, u1, hist, store):
    stress_pass(ue, 0, s, lam, mu, 2, 28, 2, 6)

    def first(i, carry):
        coefs = lane_coefs()
        for b in range(5):
            y = 4 + 8 * b
            ys = pl.ds(y, 8)
            fs = force(s, q[i, ys], i + 4, y, coefs)
            hs[i, 8 * b : 8 * b + 8] = surface(fs, 0, jnp.zeros((8, 128), F32))
            for c in range(3):
                now = ue[c, i + 4, ys]
                u1[c, i, ys] = (now - prev[c, i, ys]) + (now + fs[c])
        return carry

    lax.fori_loop(0, 24, first, 0)
    stress_pass(u1, 4, s, lam, mu, 6, 20, 6, 5)

    def second(part):
        def body(j, carry):
            i = j + 8 * part
            coefs = lane_coefs()
            for b in range(4):
                y = 8 + 8 * b
                ys = pl.ds(y, 8)
                fs = force(s, q[i + 4, ys], i + 8, y, coefs)
                r = pl.multiple_of(i * 32 + 8 * b, 8)
                hist[pl.ds(r, 8)] = surface(fs, 3, hs[i + 4, 8 * b + 4 : 8 * b + 12])
                for c in range(3):
                    now = u1[c, i + 4, ys]
                    store(part, c, j, 8 * b, (now - ue[c, i + 8, ys]) + (now + fs[c]))
            return carry

        lax.fori_loop(0, 8, body, 0)

    second(0)
    second(1)


def fill(ext, c, w, lead, parts, flags):
    center, north, south, west, east = parts
    fn, fs, fw, fe = flags
    ref = ext if lead is None else ext.at[lead]

    def row(i, f):
        ref[i, 0:8] = west(i) * (f * fw)
        ref[i, 40:48] = east(i) * (f * fe)

    for i in range(w):
        row(i, fn)
        ref[i, 8:40] = north(i) * fn
        row(16 + w + i, fs)
        ref[16 + w + i, 8:40] = south(i) * fs

    def mid(i, carry):
        row(w + i, 1.0)
        ref[w + i, 8:40] = center(i)
        return carry

    lax.fori_loop(0, 16, mid, 0)


def first_round_kernel(flags, u, p, la, mu, de, north, south, west, east, top, bot, u1, lam, muo, q, hist, ue, pe, s, hs):
    fl = [flags[0, k] for k in range(4)]
    args = (u, p, la, mu, de)
    exts = (ue, pe, lam, muo, q)
    src = 0
    off = 0
    for a, comps, w in XPARTS:
        for c in range(comps):
            arg = args[a]
            parts = (
                (lambda i, arg=arg, c=c: arg[c, i]) if comps == 3 else (lambda i, arg=arg: arg[i]),
                lambda i, src=src: north[src + i],
                lambda i, src=src: south[src + i],
                lambda i, off=off: west[off + i],
                lambda i, off=off: east[off + i],
            )
            fill(exts[a], c, w, c if comps == 3 else None, parts, fl)
            src += w
            off += 16 + 2 * w

    def scale(i, carry):
        lam[i] = lam[i] * (1.0 / 12.0)
        muo[i] = muo[i] * (1.0 / 12.0)
        return carry

    lax.fori_loop(0, 28, scale, 0)

    def invert(i, carry):
        d = q[i]
        q[i] = jnp.where(d > 0.0, (DT * DT / 12.0) / jnp.where(d > 0.0, d, 1.0), 0.0)
        return carry

    lax.fori_loop(0, 24, invert, 0)
    finish_rows(ue, pe, lam, muo, q, s, hs, u1, hist, top, bot)


def finish_rows(ue, pe, lam, mu, q, s, hs, u1, hist, top, bot):
    def store(part, c, j, y, v):
        (top, bot)[part][c, j, pl.ds(y, 8)] = v

    wave_two_steps(ue, pe, lam, mu, q, s, hs, u1, hist, store)


def fill_round(flags, top, bot, north, south, west, east, ue):
    fn, fs, fw, fe = [flags[0, k] for k in range(4)]
    for c in range(3):

        def rows(i, carry, c=c):
            ue[c, i, 0:8] = west[c, i] * (fn * fw)
            ue[c, i, 8:40] = north[c, i] * fn
            ue[c, i, 40:48] = east[c, i] * (fn * fe)
            ue[c, 8 + i, 0:8] = west[c, 8 + i] * fw
            ue[c, 8 + i, 8:40] = top[c, i]
            ue[c, 8 + i, 40:48] = east[c, 8 + i] * fe
            ue[c, 16 + i, 0:8] = west[c, 16 + i] * fw
            ue[c, 16 + i, 8:40] = bot[c, i]
            ue[c, 16 + i, 40:48] = east[c, 16 + i] * fe
            ue[c, 24 + i, 0:8] = west[c, 24 + i] * (fs * fw)
            ue[c, 24 + i, 8:40] = south[c, i] * fs
            ue[c, 24 + i, 40:48] = east[c, 24 + i] * (fs * fe)
            return carry

        lax.fori_loop(0, 8, rows, 0)


def round_kernel(flags, top, bot, north, south, west, east, prev, lam, mu, q, top2, bot2, u1, hist, ue, s, hs):
    fill_round(flags, top, bot, north, south, west, east, ue)
    finish_rows(ue, prev, lam, mu, q, s, hs, u1, hist, top2, bot2)


def last_kernel(flags, top, bot, north, south, west, east, prev, lam, mu, q, now, before, hist, ue, s, hs, u1):
    fill_round(flags, top, bot, north, south, west, east, ue)

    def store(part, c, j, y, v):
        i = j + 8 * part
        now[c, i, pl.ds(y, 8)] = v
        before[c, i, pl.ds(y, 8)] = u1[c, i + 4, pl.ds(y + 8, 8)]

    wave_two_steps(ue, prev, lam, mu, q, s, hs, u1, hist, store)


def request_kernel(tile, cell, req, key, kmod, a_ref, bhi, blo):
    ones = jnp.ones((128, 128), F32)
    sub = lax.broadcasted_iota(jnp.int32, (128, 128), 0)
    lan = lax.broadcasted_iota(jnp.int32, (128, 128), 1)
    cols = [(ones * tile[i : i + 1, :]).T for i in range(8)]
    row512 = lax.broadcasted_iota(jnp.int32, (512, 128), 0).astype(F32)
    subf = sub.astype(F32)
    for j in range(8):
        mine = tile[j : j + 1, :]
        acc = jnp.where((cols[j] == mine) & (sub < lan), 1.0, 0.0)
        for i in range(j):
            acc = acc + jnp.where(cols[i] == mine, 1.0, 0.0)
        rank = jnp.sum(acc, axis=0, keepdims=True)
        quarter = jnp.floor(rank * 0.25)
        kj = mine * 4.0 + quarter
        mj = rank - 4.0 * quarter
        key[j : j + 1, :] = kj
        kmod[j : j + 1, :] = mj
        lanes = pl.ds(128 * j, 128)
        a_ref[:, lanes] = jnp.where(row512 == kj, 1.0, 0.0).astype(BF16)
        cj = cell[j : j + 1, :]
        hi = jnp.floor(cj * (1.0 / 32.0))
        hit = subf == mj
        bhi[:, lanes] = jnp.where(hit, hi, 0.0).astype(BF16)
        blo[:, lanes] = jnp.where(hit, cj - 32.0 * hi, 0.0).astype(BF16)
    dims = (((1,), (1,)), ((), ()))
    top = lax.dot_general(a_ref[...], bhi[...], dims, preferred_element_type=F32)
    low = lax.dot_general(a_ref[...], blo[...], dims, preferred_element_type=F32)
    req[...] = (32.0 * top + low).reshape(128, 4, 128)


def answer_kernel(inc, h0, h1, h2, h3, out, hs):
    h = h0[...] + pltpu.roll(h1[...], 6, 1) + pltpu.roll(h2[...], 12, 1) + pltpu.roll(h3[...], 18, 1)
    cells = inc[...].reshape(512, 128)
    lane = lax.broadcasted_iota(jnp.int32, (512, 512), 1).astype(F32)
    acc = jnp.zeros((512, 128), F32)
    for k in range(4):
        hot = jnp.where(lane == cells[:, k : k + 1], 1.0, 0.0).astype(BF16)
        for piece in split3(pltpu.roll(h, 32 * k, 1) if k else h):
            acc = acc + jnp.dot(hot, piece, preferred_element_type=F32)
    out[...] = acc.reshape(128, 4, 128)


def building_kernel(ret, key, kmod, d_in, v_in, hf, br, st, ms, yd, cnt, d_out, v_out, h_out, pieces):
    @pl.when(pl.program_id(0) == 0)
    def _():
        full = ret[...].reshape(512, 128).T
        for n, piece in enumerate(split3(full)):
            pieces[n] = piece

    row512 = lax.broadcasted_iota(jnp.int32, (512, 128), 0).astype(F32)
    hot = jnp.where(row512 == key[0], 1.0, 0.0).astype(BF16)
    g = jnp.dot(pieces[0], hot, preferred_element_type=F32)
    g = g + jnp.dot(pieces[1], hot, preferred_element_type=F32)
    g = g + jnp.dot(pieces[2], hot, preferred_element_type=F32)
    km = kmod[0]
    ground = jnp.zeros((32, 128), F32)
    for k in range(4):
        ground = ground + jnp.where(km == k, g[32 * k : 32 * k + 32], 0.0)
    ground = ground * (1.0 / DT)
    level = lax.broadcasted_iota(jnp.int32, (64, 128), 0)
    mask = jnp.where(level < cnt[0], 1.0, 0.0)
    stiff = st[...] * mask
    yld = yd[...] * mask
    gain = DT / ms[...]
    first_row = level == 0
    last_row = level == 63

    def drift_of(x):
        return x - jnp.where(first_row, 0.0, pltpu.roll(x, 1, 0))

    for c in range(3):
        disp = d_in[c] * mask
        vel = v_in[c] * mask
        flag = br[c]
        hyst = jnp.where(flag == 1, yld, jnp.where(flag == 2, -yld, hf[c] * yld))
        drift = drift_of(disp)
        for t in range(STEPS):
            spring = stiff * (POST * drift + (1.0 - POST) * hyst)
            above = jnp.where(last_row, 0.0, pltpu.roll(spring, 63, 0))
            row = ground[3 * t + c : 3 * t + c + 1]
            vel = vel * (1.0 - DT * DAMP) + (gain * (above - spring) - mask * row)
            disp = disp + DT * vel
            new = drift_of(disp)
            hyst = jnp.minimum(jnp.maximum(hyst + new - drift, -yld), yld)
            drift = new
        d_out[c] = disp
        v_out[c] = vel
        h_out[c] = hyst


def local(u, p, de, mu, la, sd, sv, hf, br, st, ms, yd, cnt, tile, cell):
    ix = lax.axis_index("gx")
    iy = lax.axis_index("gy")
    nx = lax.axis_size("gx")
    ny = lax.axis_size("gy")
    edge = jnp.stack([ix > 0, ix < nx - 1, iy > 0, iy < ny - 1]).astype(F32).reshape(1, 4)

    up, down = pl.pallas_call(
        pack_x_kernel,
        out_shape=[sds(XPLANES, 32, 128)] * 2,
        in_specs=[HB] * 5,
        out_specs=[VM] * 2,
        scratch_shapes=[pltpu.SemaphoreType.DMA((18,))],
        compiler_params=CP,
        name="pack_x",
    )(u, p, la, mu, de)
    north = ring(up, "gx", 1)
    south = ring(down, "gx", -1)

    req, key, kmod = pl.pallas_call(
        request_kernel,
        out_shape=[sds(128, 4, 128), sds(8, 128), sds(8, 128)],
        in_specs=[VM] * 2,
        out_specs=[VM] * 3,
        scratch_shapes=[pltpu.VMEM((512, 1024), BF16), pltpu.VMEM((128, 1024), BF16), pltpu.VMEM((128, 1024), BF16)],
        compiler_params=CP,
        name="requests",
    )(tile.reshape(8, 128).astype(F32), cell.reshape(8, 128).astype(F32))
    incoming = lax.all_to_all(req, ("gx", "gy"), 0, 0, tiled=True)

    up, down = pl.pallas_call(
        pack_y_kernel,
        out_shape=[sds(YBLOCKS, 8, 128)] * 2,
        in_specs=[HB] * 5 + [VM] * 2,
        out_specs=[VM] * 2,
        scratch_shapes=[pltpu.SemaphoreType.DMA((18,))],
        compiler_params=CP,
        name="pack_y",
    )(u, p, la, mu, de, north, south)
    west = ring(up, "gy", 1)
    east = ring(down, "gy", -1)

    half = sds(3, 8, 32, 128)
    ue = pltpu.VMEM((3, 32, YR, 128), F32)
    ss = pltpu.VMEM((6, 32, YR, 128), F32)
    hh = pltpu.VMEM((24, 48, 128), F32)
    u1s = sds(3, 24, YR, 128)
    top, bot, prev, lam, mu2, q, hist = pl.pallas_call(
        first_round_kernel,
        out_shape=[half, half, u1s, sds(28, YR, 128), sds(28, YR, 128), sds(24, YR, 128), sds(512, 128)],
        in_specs=[SM] + [VM] * 9,
        out_specs=[VM] * 7,
        scratch_shapes=[ue, pltpu.VMEM((3, 24, YR, 128), F32), ss, hh],
        compiler_params=CP,
        name="wave_first",
    )(edge, u, p, la, mu, de, north, south, west, east)
    hists = [hist]
    for r in range(1, 4):
        north = ring(bot, "gx", 1)
        south = ring(top, "gx", -1)
        up, down = pl.pallas_call(
            pack_round_kernel,
            out_shape=[sds(3, 32, 8, 128)] * 2,
            in_specs=[VM] * 4,
            out_specs=[VM] * 2,
            compiler_params=CP,
            name="pack_round",
        )(top, bot, north, south)
        west = ring(up, "gy", 1)
        east = ring(down, "gy", -1)
        ins = (edge, top, bot, north, south, west, east, prev, lam, mu2, q)
        if r < 3:
            top, bot, prev, hist = pl.pallas_call(
                round_kernel,
                out_shape=[half, half, u1s, sds(512, 128)],
                in_specs=[SM] + [VM] * 10,
                out_specs=[VM] * 4,
                scratch_shapes=[ue, ss, hh],
                compiler_params=CP,
                name="wave_round",
            )(*ins)
        else:
            now, before, hist = pl.pallas_call(
                last_kernel,
                out_shape=[sds(3, 16, 32, 128)] * 2 + [sds(512, 128)],
                in_specs=[SM] + [VM] * 10,
                out_specs=[VM] * 3,
                scratch_shapes=[ue, ss, hh, pltpu.VMEM((3, 24, YR, 128), F32)],
                compiler_params=CP,
                name="wave_last",
            )(*ins)
        hists.append(hist)

    answers = pl.pallas_call(
        answer_kernel,
        out_shape=sds(128, 4, 128),
        in_specs=[VM] * 5,
        out_specs=VM,
        scratch_shapes=[pltpu.VMEM((8, 128), F32)],
        compiler_params=CP,
        name="answers",
    )(incoming, *hists)
    returned = lax.all_to_all(answers, ("gx", "gy"), 0, 0, tiled=True)

    lanes3 = pl.BlockSpec((3, 64, 128), lambda i: (0, 0, i))
    lanes2 = pl.BlockSpec((64, 128), lambda i: (0, i))
    rows = pl.BlockSpec((1, 1, 128), lambda i: (i, 0, 0))
    disp, vel, hyst = pl.pallas_call(
        building_kernel,
        out_shape=[sds(3, 64, 1024)] * 3,
        grid=(8,),
        in_specs=[pl.BlockSpec((128, 4, 128), lambda i: (0, 0, 0)), rows, rows]
        + [lanes3] * 4
        + [lanes2] * 3
        + [rows],
        out_specs=[lanes3] * 3,
        scratch_shapes=[pltpu.VMEM((3, 128, 512), BF16)],
        compiler_params=CP,
        name="buildings",
    )(
        returned,
        key.reshape(8, 1, 128),
        kmod.reshape(8, 1, 128),
        sd,
        sv,
        hf,
        br,
        st,
        ms,
        yd,
        cnt.reshape(8, 1, 128),
    )
    return now, before, disp, vel, hyst


def solution(mesh):
    grid = P(None, "gx", "gy", None)
    cells = P("gx", "gy", None)
    both = ("gx", "gy")
    b3 = P(None, None, both)
    b2 = P(None, both)
    b1 = P(both)
    return jax.shard_map(
        local,
        mesh=mesh,
        in_specs=(grid, grid, cells, cells, cells, b3, b3, b3, b3, b2, b2, b2, b1, P(both, None), b1),
        out_specs=(grid, grid, b3, b3, b3),
        check_vma=False,
    )
```

```python
import jax
import jax.numpy as jnp
from jax import lax
from jax.experimental import pallas as pl
from jax.experimental.pallas import tpu as pltpu
from jax.sharding import PartitionSpec as P

STEPS = 8
DT = 0.35
POST = 0.1
DAMP = 0.05
F32 = jnp.float32
BF16 = jnp.bfloat16
VM = pl.BlockSpec(memory_space=pltpu.VMEM)
SM = pl.BlockSpec(memory_space=pltpu.SMEM)
HB = pl.BlockSpec(memory_space=pl.ANY)
CP = pltpu.CompilerParams(vmem_limit_bytes=24 << 20)
UNROLL = 4
YR = 56

XPARTS = ((0, 3, 8), (1, 3, 4), (2, 1, 6), (3, 1, 6), (4, 1, 4))
XPLANES = sum(c * w for _, c, w in XPARTS)
YBLOCKS = sum(c * (16 + 2 * w) for _, c, w in XPARTS)


def sds(*shape):
    return jax.ShapeDtypeStruct(shape, F32)


def ring(x, axis, step):
    n = lax.axis_size(axis)
    return lax.ppermute(x, axis, [(i, (i + step) % n) for i in range(n)])


def split3(x):
    hi = x.astype(BF16)
    rest = x - hi.astype(F32)
    mid = rest.astype(BF16)
    low = (rest - mid.astype(F32)).astype(BF16)
    return hi, mid, low


def at_comp(ref, comps, c, rows, cols):
    return ref.at[c, rows, cols] if comps == 3 else ref.at[rows, cols]


def pack_x_kernel(u, p, la, mu, de, up, down, sem):
    args = (u, p, la, mu, de)
    copies = []
    off = 0
    for a, comps, w in XPARTS:
        for c in range(comps):
            full = pl.ds(0, 32)
            src_up = at_comp(args[a], comps, c, pl.ds(16 - w, w), full)
            src_dn = at_comp(args[a], comps, c, pl.ds(0, w), full)
            n = len(copies)
            copies.append(pltpu.make_async_copy(src_up, up.at[pl.ds(off, w)], sem.at[n]))
            copies.append(pltpu.make_async_copy(src_dn, down.at[pl.ds(off, w)], sem.at[n + 1]))
            off += w
    for cp in copies:
        cp.start()
    for cp in copies:
        cp.wait()


def pack_y_kernel(u, p, la, mu, de, north, south, up, down, sem):
    args = (u, p, la, mu, de)
    copies = []
    off = 0
    src = 0
    for a, comps, w in XPARTS:
        for c in range(comps):
            for dst, col in ((up, 24), (down, 0)):
                n = len(copies)
                s = at_comp(args[a], comps, c, pl.ds(0, 16), pl.ds(col, 8))
                cp = pltpu.make_async_copy(s, dst.at[pl.ds(off + w, 16)], sem.at[n])
                cp.start()
                copies.append(cp)
                dst[off : off + w] = north[src : src + w, col : col + 8]
                dst[off + w + 16 : off + 2 * w + 16] = south[src : src + w, col : col + 8]
            off += 16 + 2 * w
            src += w
    for cp in copies:
        cp.wait()


def pack_round_kernel(top, bot, north, south, up, down):
    for dst, col in ((up, 24), (down, 0)):
        dst[:, 0:8] = north[:, :, col : col + 8]
        dst[:, 8:16] = top[:, :, col : col + 8]
        dst[:, 16:24] = bot[:, :, col : col + 8]
        dst[:, 24:32] = south[:, :, col : col + 8]


def z_matrix():
    i = lax.broadcasted_iota(jnp.int32, (256, 128), 0)
    j = lax.broadcasted_iota(jnp.int32, (256, 128), 1)
    d = jnp.where(i < 128, i, i - 128) - j
    one = jnp.ones((256, 128), F32)
    near = jnp.where(d == 1, 8.0 * one, 0.0) - jnp.where(d == -1, 8.0 * one, 0.0)
    far = jnp.where(d == 2, one, 0.0) - jnp.where(d == -2, one, 0.0)
    return (near - far).astype(BF16)


def pieces2(f):
    hi = f.astype(BF16)
    lo = (f - hi.astype(F32)).astype(BF16)
    return jnp.concatenate([hi, lo], axis=1)


def dz_all(fields, mz):
    n = fields[0].shape[0]
    lhs = jnp.concatenate([pieces2(f) for f in fields], axis=0)
    out = jnp.dot(lhs, mz, preferred_element_type=F32)
    return [out[n * k : n * k + n] for k in range(len(fields))]


def dx(rows, k):
    return 8.0 * (rows[k + 3] - rows[k + 1]) - (rows[k + 4] - rows[k])


def dy(ref, c, x, y, n):
    near = ref[c, x, pl.ds(y + 1, n)] - ref[c, x, pl.ds(y - 1, n)]
    far = ref[c, x, pl.ds(y + 2, n)] - ref[c, x, pl.ds(y - 2, n)]
    return 8.0 * near - far


def stress_pass(u, ux, s, lam, mu, mz, x0, nx, y, n):
    ys = pl.ds(y, n)

    def body(i, carry):
        g0 = i * UNROLL + x0
        rows = [[u[c, g0 - ux - 2 + j, ys] for j in range(UNROLL + 4)] for c in range(3)]
        zs = dz_all([rows[c][k + 2] for k in range(UNROLL) for c in range(3)], mz[...])
        for k in range(UNROLL):
            gx = g0 + k
            x = gx - ux
            z0, z1, z2 = zs[3 * k : 3 * k + 3]
            m = mu[gx - 2, ys]
            g00 = dx(rows[0], k)
            g11 = dy(u, 1, x, y, n)
            lt = lam[gx - 2, ys] * (g00 + g11 + z2)
            m2 = m + m
            s[0, gx, ys] = lt + m2 * g00
            s[1, gx, ys] = lt + m2 * g11
            s[2, gx, ys] = lt + m2 * z2
            s[3, gx, ys] = m * (dy(u, 0, x, y, n) + dx(rows[1], k))
            s[4, gx, ys] = m * (z0 + dx(rows[2], k))
            s[5, gx, ys] = m * (z1 + dy(u, 2, x, y, n))
        return carry

    lax.fori_loop(0, nx // UNROLL, body, 0)


def forces(s, q, mz, g0, y, n):
    ys = pl.ds(y, n)
    rows = [[s[c, g0 - 2 + j, ys] for j in range(UNROLL + 4)] for c in (0, 3, 4)]
    fields = []
    for k in range(UNROLL):
        fields += [rows[2][k + 2], s[5, g0 + k, ys], s[2, g0 + k, ys]]
    zs = dz_all(fields, mz[...])
    out = []
    for k in range(UNROLL):
        x = g0 + k
        z0, z1, z2 = zs[3 * k : 3 * k + 3]
        qk = q[x - 4, ys]
        out.append(
            (
                qk * (dx(rows[0], k) + dy(s, 3, x, y, n) + z0),
                qk * (dx(rows[1], k) + dy(s, 1, x, y, n) + z1),
                qk * (dx(rows[2], k) + dy(s, 5, x, y, n) + z2),
            )
        )
    return out


def surface(fs, slot, old):
    lane = lax.broadcasted_iota(jnp.int32, fs[0].shape, 1)
    for c, f in enumerate(fs):
        v = pltpu.roll(f, slot + c, 1) if slot + c else f
        old = jnp.where(lane == slot + c, v, old)
    return old


def wave_two_steps(ue, prev, lam, mu, q, s, hs, mz, u1, hist, store):
    mz[...] = z_matrix()
    stress_pass(ue, 0, s, lam, mu, mz, 2, 28, 2, 48)

    def first(start, count, stride, seen):
        def body(j, carry):
            i0 = start + j * stride
            for k, fs in enumerate(forces(s, q, mz, i0 + 4, 4, 48)):
                i = i0 + k
                if seen:
                    hs[i - 4] = surface(fs, 0, jnp.zeros((48, 128), F32))
                for c in range(3):
                    now = ue[c, i + 4, 4:52]
                    u1[c, i, 4:52] = (now - prev[c, i, 4:52]) + (now + fs[c])
            return carry

        lax.fori_loop(0, count, body, 0)

    first(0, 2, 20, False)
    first(4, 16 // UNROLL, UNROLL, True)
    if UNROLL == 2:
        first(2, 2, 20, False)
    stress_pass(u1, 4, s, lam, mu, mz, 6, 20, 6, 48)

    def second(part):
        def body(j0, carry):
            i0 = j0 * UNROLL + 8 * part
            for k, fs in enumerate(forces(s, q, mz, i0 + 8, 8, 32)):
                i = i0 + k
                r = pl.multiple_of(i * 32, 32)
                hist[pl.ds(r, 32)] = surface(fs, 3, hs[i, 4:36])
                for c in range(3):
                    now = u1[c, i + 4, 8:40]
                    store(part, c, j0 * UNROLL + k, (now - ue[c, i + 8, 8:40]) + (now + fs[c]))
            return carry

        lax.fori_loop(0, 8 // UNROLL, body, 0)

    second(0)
    second(1)


def fill(ext, c, w, lead, parts, flags):
    center, north, south, west, east = parts
    fn, fs, fw, fe = flags
    ref = ext if lead is None else ext.at[lead]

    def row(i, f):
        ref[i, 0:8] = west(i) * (f * fw)
        ref[i, 40:48] = east(i) * (f * fe)

    for i in range(w):
        row(i, fn)
        ref[i, 8:40] = north(i) * fn
        row(16 + w + i, fs)
        ref[16 + w + i, 8:40] = south(i) * fs

    def mid(i, carry):
        row(w + i, 1.0)
        ref[w + i, 8:40] = center(i)
        return carry

    lax.fori_loop(0, 16, mid, 0)


def first_round_kernel(flags, u, p, la, mu, de, north, south, west, east, top, bot, u1, lam, muo, q, hist, ue, pe, s, hs, mz):
    fl = [flags[0, k] for k in range(4)]
    args = (u, p, la, mu, de)
    exts = (ue, pe, lam, muo, q)
    src = 0
    off = 0
    for a, comps, w in XPARTS:
        for c in range(comps):
            arg = args[a]
            parts = (
                (lambda i, arg=arg, c=c: arg[c, i]) if comps == 3 else (lambda i, arg=arg: arg[i]),
                lambda i, src=src: north[src + i],
                lambda i, src=src: south[src + i],
                lambda i, off=off: west[off + i],
                lambda i, off=off: east[off + i],
            )
            fill(exts[a], c, w, c if comps == 3 else None, parts, fl)
            src += w
            off += 16 + 2 * w

    def scale(i, carry):
        lam[i] = lam[i] * (1.0 / 12.0)
        muo[i] = muo[i] * (1.0 / 12.0)
        return carry

    lax.fori_loop(0, 28, scale, 0)

    def invert(i, carry):
        d = q[i]
        q[i] = jnp.where(d > 0.0, (DT * DT / 12.0) / jnp.where(d > 0.0, d, 1.0), 0.0)
        return carry

    lax.fori_loop(0, 24, invert, 0)
    finish_rows(ue, pe, lam, muo, q, s, hs, mz, u1, hist, top, bot)


def finish_rows(ue, pe, lam, mu, q, s, hs, mz, u1, hist, top, bot):
    def store(part, c, j, v):
        (top, bot)[part][c, j] = v

    wave_two_steps(ue, pe, lam, mu, q, s, hs, mz, u1, hist, store)


def fill_round(flags, top, bot, north, south, west, east, ue):
    fn, fs, fw, fe = [flags[0, k] for k in range(4)]
    for c in range(3):

        def rows(i, carry, c=c):
            ue[c, i, 0:8] = west[c, i] * (fn * fw)
            ue[c, i, 8:40] = north[c, i] * fn
            ue[c, i, 40:48] = east[c, i] * (fn * fe)
            ue[c, 8 + i, 0:8] = west[c, 8 + i] * fw
            ue[c, 8 + i, 8:40] = top[c, i]
            ue[c, 8 + i, 40:48] = east[c, 8 + i] * fe
            ue[c, 16 + i, 0:8] = west[c, 16 + i] * fw
            ue[c, 16 + i, 8:40] = bot[c, i]
            ue[c, 16 + i, 40:48] = east[c, 16 + i] * fe
            ue[c, 24 + i, 0:8] = west[c, 24 + i] * (fs * fw)
            ue[c, 24 + i, 8:40] = south[c, i] * fs
            ue[c, 24 + i, 40:48] = east[c, 24 + i] * (fs * fe)
            return carry

        lax.fori_loop(0, 8, rows, 0)


def round_kernel(flags, top, bot, north, south, west, east, prev, lam, mu, q, top2, bot2, u1, hist, ue, s, hs, mz):
    fill_round(flags, top, bot, north, south, west, east, ue)
    finish_rows(ue, prev, lam, mu, q, s, hs, mz, u1, hist, top2, bot2)


def last_kernel(flags, top, bot, north, south, west, east, prev, lam, mu, q, now, before, hist, ue, s, hs, mz, u1):
    fill_round(flags, top, bot, north, south, west, east, ue)

    def store(part, c, j, v):
        i = j + 8 * part
        now[c, i] = v
        before[c, i] = u1[c, i + 4, 8:40]

    wave_two_steps(ue, prev, lam, mu, q, s, hs, mz, u1, hist, store)


def request_kernel(tile, cell, req, key, kmod, a_ref, bhi, blo):
    ones = jnp.ones((128, 128), F32)
    sub = lax.broadcasted_iota(jnp.int32, (128, 128), 0)
    lan = lax.broadcasted_iota(jnp.int32, (128, 128), 1)
    cols = [(ones * tile[i : i + 1, :]).T for i in range(8)]
    row512 = lax.broadcasted_iota(jnp.int32, (512, 128), 0).astype(F32)
    subf = sub.astype(F32)
    for j in range(8):
        mine = tile[j : j + 1, :]
        acc = jnp.where((cols[j] == mine) & (sub < lan), 1.0, 0.0)
        for i in range(j):
            acc = acc + jnp.where(cols[i] == mine, 1.0, 0.0)
        rank = jnp.sum(acc, axis=0, keepdims=True)
        quarter = jnp.floor(rank * 0.25)
        kj = mine * 4.0 + quarter
        mj = rank - 4.0 * quarter
        key[j : j + 1, :] = kj
        kmod[j : j + 1, :] = mj
        lanes = pl.ds(128 * j, 128)
        a_ref[:, lanes] = jnp.where(row512 == kj, 1.0, 0.0).astype(BF16)
        cj = cell[j : j + 1, :]
        hi = jnp.floor(cj * (1.0 / 32.0))
        hit = subf == mj
        bhi[:, lanes] = jnp.where(hit, hi, 0.0).astype(BF16)
        blo[:, lanes] = jnp.where(hit, cj - 32.0 * hi, 0.0).astype(BF16)
    dims = (((1,), (1,)), ((), ()))
    top = lax.dot_general(a_ref[...], bhi[...], dims, preferred_element_type=F32)
    low = lax.dot_general(a_ref[...], blo[...], dims, preferred_element_type=F32)
    req[...] = (32.0 * top + low).reshape(128, 4, 128)


def hot_kernel(inc, hot):
    cells = inc[...].reshape(512, 128)
    lane = lax.broadcasted_iota(jnp.int32, (512, 512), 1).astype(F32)
    for k in range(4):
        hot[k] = jnp.where(lane == cells[:, k : k + 1], 1.0, 0.0).astype(BF16)


def pick(h, hot):
    acc = jnp.zeros((512, 128), F32)
    for k in range(4):
        hk = pltpu.roll(h, 32 * k, 1) if k else h
        hi = hk.astype(BF16)
        mid = (hk - hi.astype(F32)).astype(BF16)
        both = jnp.dot(hot[k], jnp.concatenate([hi, mid], axis=1), preferred_element_type=F32)
        acc = acc + (both[:, :128] + both[:, 128:])
    return acc


def early_answer_kernel(hot, h0, h1, h2, out):
    h = h0[...] + pltpu.roll(h1[...], 6, 1) + pltpu.roll(h2[...], 12, 1)
    out[...] = pick(h, hot)


def answer_kernel(hot, early, h3, out):
    out[...] = (early[...] + pick(pltpu.roll(h3[...], 18, 1), hot)).reshape(128, 4, 128)


def building_start_kernel(d_in, v_in, hf, br, st, ms, yd, cnt, disp, vel, hyst, stiff, yld, gain):
    level = lax.broadcasted_iota(jnp.int32, (64, 128), 0)
    mask = jnp.where(level < cnt[0], 1.0, 0.0)
    y = yd[...] * mask
    stiff[...] = st[...] * mask
    yld[...] = y
    gain[...] = DT / ms[...]
    for c in range(3):
        disp[c] = d_in[c] * mask
        vel[c] = v_in[c] * mask
        flag = br[c]
        hyst[c] = jnp.where(flag == 1, y, jnp.where(flag == 2, -y, hf[c] * y))


def building_kernel(ret, key, kmod, cnt, d_in, v_in, h_in, st, yd, gn, d_out, v_out, h_out, ground, bufs, sem):
    pieces = split3(ret[...].reshape(512, 128).T)[:2]
    row512 = lax.broadcasted_iota(jnp.int32, (512, 128), 0).astype(F32)
    for j in range(8):
        lanes = pl.ds(128 * j, 128)
        hot = jnp.where(row512 == key[j : j + 1, :], 1.0, 0.0).astype(BF16)
        g = jnp.dot(pieces[0], hot, preferred_element_type=F32)
        g = g + jnp.dot(pieces[1], hot, preferred_element_type=F32)
        km = kmod[j : j + 1, :]
        acc = jnp.zeros((32, 128), F32)
        for k in range(4):
            acc = acc + jnp.where(km == k, g[32 * k : 32 * k + 32], 0.0)
        ground[:, lanes] = acc * (1.0 / DT)
    outs = (d_out, v_out, h_out)
    copies = []
    for c in range(3):

        def chunk(j, carry, c=c):
            lanes = pl.ds(pl.multiple_of(j * 128, 128), 128)
            level = lax.broadcasted_iota(jnp.int32, (64, 128), 0)
            first_row = level == 0
            last_row = level == 63
            mask = jnp.where(level < cnt[0:1, lanes], 1.0, 0.0)

            def drift_of(x):
                return x - jnp.where(first_row, 0.0, pltpu.roll(x, 1, 0))

            stiff = st[:, lanes]
            yld = yd[:, lanes]
            gain = gn[:, lanes]
            disp = d_in[c, :, lanes]
            vel = v_in[c, :, lanes]
            hyst = h_in[c, :, lanes]
            drift = drift_of(disp)
            for t in range(STEPS):
                spring = stiff * (POST * drift + (1.0 - POST) * hyst)
                above = jnp.where(last_row, 0.0, pltpu.roll(spring, 63, 0))
                row = ground[3 * t + c : 3 * t + c + 1, lanes]
                vel = vel * (1.0 - DT * DAMP) + (gain * (above - spring) - mask * row)
                disp = disp + DT * vel
                new = drift_of(disp)
                hyst = jnp.minimum(jnp.maximum(hyst + new - drift, -yld), yld)
                drift = new
            bufs[0, c, :, lanes] = disp
            bufs[1, c, :, lanes] = vel
            bufs[2, c, :, lanes] = hyst
            return carry

        lax.fori_loop(0, 8, chunk, 0)
        for n in range(3):
            cp = pltpu.make_async_copy(bufs.at[n, c], outs[n].at[c], sem.at[3 * c + n])
            cp.start()
            copies.append(cp)
    for cp in copies:
        cp.wait()


def building_start(sd, sv, hf, br, st, ms, yd, cnt):
    lanes3 = pl.BlockSpec((3, 64, 128), lambda i: (0, 0, i))
    lanes2 = pl.BlockSpec((64, 128), lambda i: (0, i))
    rows = pl.BlockSpec((1, 1, 128), lambda i: (i, 0, 0))
    return pl.pallas_call(
        building_start_kernel,
        out_shape=[sds(3, 64, 1024)] * 3 + [sds(64, 1024)] * 3,
        grid=(8,),
        in_specs=[lanes3] * 4 + [lanes2] * 3 + [rows],
        out_specs=[lanes3] * 3 + [lanes2] * 3,
        compiler_params=CP,
        name="building_start",
    )(sd, sv, hf, br, st, ms, yd, cnt.reshape(8, 1, 128))


def local(u, p, de, mu, la, sd, sv, hf, br, st, ms, yd, cnt, tile, cell):
    ix = lax.axis_index("gx")
    iy = lax.axis_index("gy")
    nx = lax.axis_size("gx")
    ny = lax.axis_size("gy")
    edge = jnp.stack([ix > 0, ix < nx - 1, iy > 0, iy < ny - 1]).astype(F32).reshape(1, 4)

    up, down = pl.pallas_call(
        pack_x_kernel,
        out_shape=[sds(XPLANES, 32, 128)] * 2,
        in_specs=[HB] * 5,
        out_specs=[VM] * 2,
        scratch_shapes=[pltpu.SemaphoreType.DMA((18,))],
        compiler_params=CP,
        name="pack_x",
    )(u, p, la, mu, de)
    north = ring(up, "gx", 1)
    south = ring(down, "gx", -1)

    req, key, kmod = pl.pallas_call(
        request_kernel,
        out_shape=[sds(128, 4, 128), sds(8, 128), sds(8, 128)],
        in_specs=[VM] * 2,
        out_specs=[VM] * 3,
        scratch_shapes=[pltpu.VMEM((512, 1024), BF16), pltpu.VMEM((128, 1024), BF16), pltpu.VMEM((128, 1024), BF16)],
        compiler_params=CP,
        name="requests",
    )(tile.reshape(8, 128).astype(F32), cell.reshape(8, 128).astype(F32))
    incoming = lax.all_to_all(req, ("gx", "gy"), 0, 0, tiled=True)
    north, south, incoming = lax.optimization_barrier((north, south, incoming))

    up, down = pl.pallas_call(
        pack_y_kernel,
        out_shape=[sds(YBLOCKS, 8, 128)] * 2,
        in_specs=[HB] * 5 + [VM] * 2,
        out_specs=[VM] * 2,
        scratch_shapes=[pltpu.SemaphoreType.DMA((18,))],
        compiler_params=CP,
        name="pack_y",
    )(u, p, la, mu, de, north, south)
    west = ring(up, "gy", 1)
    east = ring(down, "gy", -1)

    half = sds(3, 8, 32, 128)
    ue = pltpu.VMEM((3, 32, YR, 128), F32)
    ss = pltpu.VMEM((6, 32, YR, 128), F32)
    hh = pltpu.VMEM((16, 48, 128), F32)
    mz = pltpu.VMEM((256, 128), BF16)
    u1s = sds(3, 24, YR, 128)
    top, bot, prev, lam, mu2, q, hist = pl.pallas_call(
        first_round_kernel,
        out_shape=[half, half, u1s, sds(28, YR, 128), sds(28, YR, 128), sds(24, YR, 128), sds(512, 128)],
        in_specs=[SM] + [VM] * 9,
        out_specs=[VM] * 7,
        scratch_shapes=[ue, pltpu.VMEM((3, 24, YR, 128), F32), ss, hh, mz],
        compiler_params=CP,
        name="wave_first",
    )(edge, u, p, la, mu, de, north, south, west, east)
    hists = [hist]
    for r in range(1, 4):
        north = ring(bot, "gx", 1)
        south = ring(top, "gx", -1)
        if r == 1:
            starts = building_start(sd, sv, hf, br, st, ms, yd, cnt)
            hot = pl.pallas_call(
                hot_kernel,
                out_shape=jax.ShapeDtypeStruct((4, 512, 512), BF16),
                in_specs=[VM],
                out_specs=VM,
                compiler_params=CP,
                name="hot",
            )(incoming)
            north, south, hot, starts = lax.optimization_barrier((north, south, hot, starts))
        up, down = pl.pallas_call(
            pack_round_kernel,
            out_shape=[sds(3, 32, 8, 128)] * 2,
            in_specs=[VM] * 4,
            out_specs=[VM] * 2,
            compiler_params=CP,
            name="pack_round",
        )(top, bot, north, south)
        west = ring(up, "gy", 1)
        east = ring(down, "gy", -1)
        if r == 3:
            early = pl.pallas_call(
                early_answer_kernel,
                out_shape=sds(512, 128),
                in_specs=[VM] * 4,
                out_specs=VM,
                compiler_params=CP,
                name="early_answers",
            )(hot, *hists)
            west, east, early = lax.optimization_barrier((west, east, early))
        ins = (edge, top, bot, north, south, west, east, prev, lam, mu2, q)
        if r < 3:
            top, bot, prev, hist = pl.pallas_call(
                round_kernel,
                out_shape=[half, half, u1s, sds(512, 128)],
                in_specs=[SM] + [VM] * 10,
                out_specs=[VM] * 4,
                scratch_shapes=[ue, ss, hh, mz],
                compiler_params=CP,
                name="wave_round",
            )(*ins)
        else:
            now, before, hist = pl.pallas_call(
                last_kernel,
                out_shape=[sds(3, 16, 32, 128)] * 2 + [sds(512, 128)],
                in_specs=[SM] + [VM] * 10,
                out_specs=[VM] * 3,
                scratch_shapes=[ue, ss, hh, mz, pltpu.VMEM((3, 24, YR, 128), F32)],
                compiler_params=CP,
                name="wave_last",
            )(*ins)
        hists.append(hist)

    answers = pl.pallas_call(
        answer_kernel,
        out_shape=sds(128, 4, 128),
        in_specs=[VM] * 3,
        out_specs=VM,
        compiler_params=CP,
        name="answers",
    )(hot, early, hists[3])
    returned = lax.all_to_all(answers, ("gx", "gy"), 0, 0, tiled=True)
    disp, vel, hyst = pl.pallas_call(
        building_kernel,
        out_shape=[sds(3, 64, 1024)] * 3,
        in_specs=[VM] * 10,
        out_specs=[HB] * 3,
        scratch_shapes=[
            pltpu.VMEM((32, 1024), F32),
            pltpu.VMEM((3, 3, 64, 1024), F32),
            pltpu.SemaphoreType.DMA((9,)),
        ],
        compiler_params=CP,
        name="buildings",
    )(returned, key, kmod, cnt.reshape(1, 1024), *starts)
    return now, before, disp, vel, hyst


def solution(mesh):
    grid = P(None, "gx", "gy", None)
    cells = P("gx", "gy", None)
    both = ("gx", "gy")
    b3 = P(None, None, both)
    b2 = P(None, both)
    b1 = P(both)
    return jax.shard_map(
        local,
        mesh=mesh,
        in_specs=(grid, grid, cells, cells, cells, b3, b3, b3, b3, b2, b2, b2, b1, P(both, None), b1),
        out_specs=(grid, grid, b3, b3, b3),
        check_vma=False,
    )
```

```python
import jax
import jax.numpy as jnp
from jax import lax
from jax.experimental import pallas as pl
from jax.experimental.pallas import tpu as pltpu
from jax.sharding import PartitionSpec as P

STEPS = 8
DT = 0.35
POST = 0.1
DAMP = 0.05
F32 = jnp.float32
BF16 = jnp.bfloat16
VM = pl.BlockSpec(memory_space=pltpu.VMEM)
SM = pl.BlockSpec(memory_space=pltpu.SMEM)
HB = pl.BlockSpec(memory_space=pltpu.HBM)
CP = pltpu.CompilerParams(vmem_limit_bytes=12 << 20)
YR = 56

XPARTS = ((0, 3, 8), (1, 3, 4), (2, 1, 6), (3, 1, 6), (4, 1, 4))
XPLANES = sum(c * w for _, c, w in XPARTS)


def sds(*shape):
    return jax.ShapeDtypeStruct(shape, F32)


def ring(x, axis, step):
    n = lax.axis_size(axis)
    return lax.ppermute(x, axis, [(i, (i + step) % n) for i in range(n)])


def split3(x):
    hi = x.astype(BF16)
    rest = x - hi.astype(F32)
    mid = rest.astype(BF16)
    low = (rest - mid.astype(F32)).astype(BF16)
    return hi, mid, low


def at_comp(ref, comps, c, rows, cols):
    return ref.at[c, rows, cols] if comps == 3 else ref.at[rows, cols]


def pack_first_kernel(u, p, la, mu, de, up, down, right, left, sem):
    args = (u, p, la, mu, de)
    copies = []
    off = 0
    row = 0
    for a, comps, w in XPARTS:
        for c in range(comps):
            full = pl.ds(0, 32)
            every = pl.ds(0, 16)
            for src, dst in (
                (at_comp(args[a], comps, c, pl.ds(16 - w, w), full), up.at[pl.ds(off, w)]),
                (at_comp(args[a], comps, c, pl.ds(0, w), full), down.at[pl.ds(off, w)]),
                (at_comp(args[a], comps, c, every, pl.ds(24, 8)), right.at[pl.ds(row, 16)]),
                (at_comp(args[a], comps, c, every, pl.ds(0, 8)), left.at[pl.ds(row, 16)]),
            ):
                cp = pltpu.make_async_copy(src, dst, sem.at[len(copies)])
                cp.start()
                copies.append(cp)
            off += w
            row += 16
    for cp in copies:
        cp.wait()


def pack_corner_kernel(north, south, right, left):
    for dst, col in ((right, 24), (left, 0)):
        dst[0] = north[:, col : col + 8]
        dst[1] = south[:, col : col + 8]


def z_matrix():
    i = lax.broadcasted_iota(jnp.int32, (256, 128), 0)
    j = lax.broadcasted_iota(jnp.int32, (256, 128), 1)
    d = jnp.where(i < 128, i, i - 128) - j
    one = jnp.ones((256, 128), F32)
    near = jnp.where(d == 1, 8.0 * one, 0.0) - jnp.where(d == -1, 8.0 * one, 0.0)
    far = jnp.where(d == 2, one, 0.0) - jnp.where(d == -2, one, 0.0)
    return (near - far).astype(BF16)


def pieces2(f):
    hi = f.astype(BF16)
    lo = (f - hi.astype(F32)).astype(BF16)
    return jnp.concatenate([hi, lo], axis=1)


def dz_all(fields, mz):
    n = fields[0].shape[0]
    lhs = pieces2(jnp.concatenate(fields, axis=0))
    out = jnp.dot(lhs, mz, preferred_element_type=F32)
    return [out[n * k : n * k + n] for k in range(len(fields))]


def dx(rows, k):
    return 8.0 * (rows[k + 3] - rows[k + 1]) - (rows[k + 4] - rows[k])


def dy(ref, c, x, y, n):
    near = ref[c, x, pl.ds(y + 1, n)] - ref[c, x, pl.ds(y - 1, n)]
    far = ref[c, x, pl.ds(y + 2, n)] - ref[c, x, pl.ds(y - 2, n)]
    return 8.0 * near - far


def for_x(count, fn):
    def body(i, carry):
        fn(i)
        return carry

    lax.fori_loop(0, count, body, 0)


def stress_rows(u, ux, s, sx, lam, mu, mz, blocks, m, n):
    rows = []
    fields = []
    for g0, y in blocks:
        r = [[u[c, g0 - ux - 2 + j, pl.ds(y, n)] for j in range(m + 4)] for c in range(3)]
        rows.append(r)
        fields += [r[c][k + 2] for k in range(m) for c in range(3)]
    zs = dz_all(fields, mz[...])
    for (g0, y), r in zip(blocks, rows):
        ys = pl.ds(y, n)
        for k in range(m):
            gx = g0 + k
            x = gx - ux
            z0, z1, z2 = zs[:3]
            zs = zs[3:]
            mm = mu[gx - 2, ys]
            g00 = dx(r[0], k)
            g11 = dy(u, 1, x, y, n)
            lt = lam[gx - 2, ys] * (g00 + g11 + z2)
            m2 = mm + mm
            s[0, gx - sx, ys] = lt + m2 * g00
            s[1, gx - sx, ys] = lt + m2 * g11
            s[2, gx - sx, ys] = lt + m2 * z2
            s[3, gx - sx, ys] = mm * (dy(u, 0, x, y, n) + dx(r[1], k))
            s[4, gx - sx, ys] = mm * (z0 + dx(r[2], k))
            s[5, gx - sx, ys] = mm * (z1 + dy(u, 2, x, y, n))


def forces(s, sx, q, mz, blocks, m, n):
    rows = []
    fields = []
    for g0, y in blocks:
        ys = pl.ds(y, n)
        r = [[s[c, g0 - sx - 2 + j, ys] for j in range(m + 4)] for c in (0, 3, 4)]
        rows.append(r)
        for k in range(m):
            fields += [r[2][k + 2], s[5, g0 - sx + k, ys], s[2, g0 - sx + k, ys]]
    zs = dz_all(fields, mz[...])
    out = []
    for (g0, y), r in zip(blocks, rows):
        mine = []
        for k in range(m):
            x = g0 + k
            z0, z1, z2 = zs[:3]
            zs = zs[3:]
            qk = q[x - 4, pl.ds(y, n)]
            mine.append(
                (
                    qk * (dx(r[0], k) + dy(s, 3, x - sx, y, n) + z0),
                    qk * (dx(r[1], k) + dy(s, 1, x - sx, y, n) + z1),
                    qk * (dx(r[2], k) + dy(s, 5, x - sx, y, n) + z2),
                )
            )
        out.append(mine)
    return out


def surface(fs, slot, old):
    lane = lax.broadcasted_iota(jnp.int32, fs[0].shape, 1)
    for c, f in enumerate(fs):
        v = pltpu.roll(f, slot + c, 1) if slot + c else f
        old = jnp.where(lane == slot + c, v, old)
    return old


def first_rows(ue, prev, q, s, hs, mz, u1, blocks, m, n, seen):
    for (i0, y), fr in zip(blocks, forces(s, 2, q, mz, [(i0 + 4, y) for i0, y in blocks], m, n)):
        ys = pl.ds(y, n)
        for k, fs in enumerate(fr):
            i = i0 + k
            if k in seen(i0):
                hs[i - 4, pl.ds(y - 4, n)] = surface(fs, 0, jnp.zeros((n, 128), F32))
            for c in range(3):
                now = ue[c, i + 4, ys]
                u1[c, i, ys] = (now - prev[c, i, ys]) + (now + fs[c])


def second_rows(ue, q, s, hs, mz, u1, hist, blocks, m, n):
    places = [(j0 + 8 * part + 8, y) for _, j0, part, y, _ in blocks]
    for (out, j0, part, y, side), fr in zip(blocks, forces(s, 6, q, mz, places, m, n)):
        ys = pl.ds(y, n)
        for k, fs in enumerate(fr):
            i = j0 + 8 * part + k
            r = pl.multiple_of(i * 32 + y - 8, 8)
            hist[pl.ds(r, n)] = surface(fs, 3, hs[i, pl.ds(y - 4, n)])
            for c in range(3):
                now = u1[c, i + 4, ys]
                v = (now - ue[c, i + 8, ys]) + (now + fs[c])
                out[c, j0 + k, pl.ds(y - 8, n)] = v
                if side is not None:
                    side[c, i] = v


def two_steps(prev, lam, mu, q, ue, s, s2, hs, u1, top, bot, hist, mz):
    mz[...] = z_matrix()
    none = lambda i0: ()
    every = lambda i0: range(4)
    for_x(7, lambda i: stress_rows(ue, 0, s, 2, lam, mu, mz, [(4 * i + 2, 2)], 4, 48))
    for_x(2, lambda i: first_rows(ue, prev, q, s, hs, mz, u1, [(20 * i, 4)], 4, 48, none))
    for_x(4, lambda i: first_rows(ue, prev, q, s, hs, mz, u1, [(4 * i + 4, 4)], 4, 48, every))
    for_x(5, lambda i: stress_rows(u1, 4, s2, 6, lam, mu, mz, [(4 * i + 6, 6)], 4, 48))
    for part, out in enumerate((top, bot)):
        for_x(2, lambda i: second_rows(ue, q, s2, hs, mz, u1, hist, [(out, 4 * i, part, 8, None)], 4, 32))


def patch_two_steps(prev, lam, mu, q, ue, s, s2, hs, u1, top, bot, hist, right, left, mz):
    mz[...] = z_matrix()
    stress_rows(ue, 0, s, 2, lam, mu, mz, [(x, y) for x in (2, 22) for y in (2, 38)], 8, 8)
    seen = lambda i0: range(4, 8) if i0 == 0 else range(4)
    first_rows(ue, prev, q, s, hs, mz, u1, [(i, y) for i in (0, 16) for y in (4, 36)], 8, 8, seen)
    stress_rows(u1, 4, s2, 6, lam, mu, mz, [(x, y) for x in (6, 18) for y in (6, 34)], 8, 8)
    blocks = [(o, 0, part, y, side) for part, o in enumerate((top, bot)) for y, side in ((8, left), (32, right))]
    second_rows(ue, q, s2, hs, mz, u1, hist, blocks, 8, 8)


def first_round_kernel(flags, u, p, la, mu, de, north, south, west, east, ue, s, s2, hs, u1, top, bot, hist, pe, lam, muo, q, mz, sem):
    fn, fs, fw, fe = [flags[0, k] for k in range(4)]
    copies = []
    args = (u, p, la, mu, de)
    exts = (ue, pe, lam, muo, q)
    off = 0
    row = 0
    for a, comps, w in XPARTS:
        for c in range(comps):
            ref = exts[a].at[c] if comps == 3 else exts[a]
            arg = args[a].at[c] if comps == 3 else args[a]
            cp = pltpu.make_async_copy(arg, ref.at[pl.ds(w, 16), pl.ds(8, 32)], sem.at[len(copies)])
            cp.start()
            copies.append(cp)
            none = jnp.zeros((8, 128), F32)
            for i in range(w):
                for x, strip, f in ((i, north, fn), (16 + w + i, south, fs)):
                    ref[x, 0:8] = none
                    ref[x, 8:40] = strip[off + i] * f
                    ref[x, 40:48] = none

            def mid(i, ref=ref, row=row, w=w):
                ref[w + i, 0:8] = west[row + i] * fw
                ref[w + i, 40:48] = east[row + i] * fe

            for_x(16, mid)
            off += w
            row += 16

    for cp in copies:
        cp.wait()

    def scale(i):
        lam[i, 0:48] = lam[i, 0:48] * (1.0 / 12.0)
        muo[i, 0:48] = muo[i, 0:48] * (1.0 / 12.0)

    for_x(28, scale)

    def invert(i):
        q[i, 0:48] = inverse_density(q[i, 0:48])

    for_x(24, invert)
    two_steps(pe, lam, muo, q, ue, s, s2, hs, u1, top, bot, hist, mz)


def inverse_density(d):
    return jnp.where(d > 0.0, (DT * DT / 12.0) / jnp.where(d > 0.0, d, 1.0), 0.0)


def first_patch_kernel(*refs):
    flags, wc, ec = refs[:3]
    ue, s, s2, hs, u1, top, bot, hist, pe, lam, mu, q, right, left, mz = refs[15:]
    fn, fs, fw, fe = [flags[0, k] for k in range(4)]
    exts = (ue, pe, lam, mu, q)
    off = 0
    for a, comps, w in XPARTS:
        for c in range(comps):
            ref = exts[a].at[c] if comps == 3 else exts[a]
            for i in range(w):
                for half, x, f in ((0, i, fn), (1, 16 + w + i, fs)):
                    for strip, y, g in ((wc, 0, fw), (ec, 40, fe)):
                        v = strip[half, off + i] * (f * g)
                        if a in (2, 3):
                            v = v * (1.0 / 12.0)
                        ref[x, y : y + 8] = inverse_density(v) if a == 4 else v
            off += w
    patch_two_steps(pe, lam, mu, q, ue, s, s2, hs, u1, top, bot, hist, right, left, mz)


def round_kernel(flags, top, bot, north, south, west, east, prev, lam, mu, q, ue, s, s2, hs, u1, top2, bot2, hist, mz):
    fn, fs, fw, fe = [flags[0, k] for k in range(4)]
    none = jnp.zeros((8, 128), F32)
    for c in range(3):

        def rows(i, c=c):
            for x, strip, f in ((i, north, fn), (24 + i, south, fs)):
                ue[c, x, 0:8] = none
                ue[c, x, 8:40] = strip[8 * c + i] * f
                ue[c, x, 40:48] = none
            for x, strip in ((i, top), (8 + i, bot)):
                ue[c, 8 + x, 0:8] = west[c, x] * fw
                ue[c, 8 + x, 8:40] = strip[c, i]
                ue[c, 8 + x, 40:48] = east[c, x] * fe

        for_x(8, rows)
    two_steps(prev, lam, mu, q, ue, s, s2, hs, u1, top2, bot2, hist, mz)


def fill_corners(flags, wc, ec, ue):
    fn, fs, fw, fe = [flags[0, k] for k in range(4)]
    for c in range(3):

        def rows(i, c=c):
            for half, x, f in ((0, i, fn), (1, 24 + i, fs)):
                ue[c, x, 0:8] = wc[half, 8 * c + i] * (f * fw)
                ue[c, x, 40:48] = ec[half, 8 * c + i] * (f * fe)

        for_x(8, rows)


def patch_kernel(*refs):
    flags, wc, ec, prev, lam, mu, q = refs[:7]
    ue, s, s2, hs, u1, top, bot, hist, right, left, mz = refs[15:]
    fill_corners(flags, wc, ec, ue)
    patch_two_steps(prev, lam, mu, q, ue, s, s2, hs, u1, top, bot, hist, right, left, mz)


def last_patch_kernel(*refs):
    flags, wc, ec, prev, lam, mu, q = refs[:7]
    ue, s, s2, hs, u1, top, bot, hist, now, before, right, left, mz = refs[15:]
    fill_corners(flags, wc, ec, ue)
    patch_two_steps(prev, lam, mu, q, ue, s, s2, hs, u1, top, bot, hist, right, left, mz)
    for c in range(3):

        def rows(i, c=c):
            now[c, i] = top[c, i]
            now[c, 8 + i] = bot[c, i]
            before[c, i] = u1[c, i + 4, 8:40]
            before[c, 8 + i] = u1[c, i + 12, 8:40]

        for_x(8, rows)


def request_kernel(tile, cell, req, key, kmod, a_ref, bhi, blo):
    ones = jnp.ones((128, 128), F32)
    sub = lax.broadcasted_iota(jnp.int32, (128, 128), 0)
    lan = lax.broadcasted_iota(jnp.int32, (128, 128), 1)
    cols = [(ones * tile[i : i + 1, :]).T for i in range(8)]
    row512 = lax.broadcasted_iota(jnp.int32, (512, 128), 0).astype(F32)
    subf = sub.astype(F32)
    for j in range(8):
        mine = tile[j : j + 1, :]
        acc = jnp.where((cols[j] == mine) & (sub < lan), 1.0, 0.0)
        for i in range(j):
            acc = acc + jnp.where(cols[i] == mine, 1.0, 0.0)
        rank = jnp.sum(acc, axis=0, keepdims=True)
        quarter = jnp.floor(rank * 0.25)
        kj = mine * 4.0 + quarter
        mj = rank - 4.0 * quarter
        key[j : j + 1, :] = kj
        kmod[j : j + 1, :] = mj
        lanes = pl.ds(128 * j, 128)
        a_ref[:, lanes] = jnp.where(row512 == kj, 1.0, 0.0).astype(BF16)
        cj = cell[j : j + 1, :]
        hi = jnp.floor(cj * (1.0 / 32.0))
        hit = subf == mj
        bhi[:, lanes] = jnp.where(hit, hi, 0.0).astype(BF16)
        blo[:, lanes] = jnp.where(hit, cj - 32.0 * hi, 0.0).astype(BF16)
    dims = (((1,), (1,)), ((), ()))
    top = lax.dot_general(a_ref[...], bhi[...], dims, preferred_element_type=F32)
    low = lax.dot_general(a_ref[...], blo[...], dims, preferred_element_type=F32)
    req[...] = (32.0 * top + low).reshape(128, 4, 128)


def hot_kernel(inc, hot):
    cells = inc[...].reshape(512, 128)
    lane = lax.broadcasted_iota(jnp.int32, (512, 512), 1).astype(F32)
    for k in range(4):
        hot[k] = jnp.where(lane == cells[:, k : k + 1], 1.0, 0.0).astype(BF16)


def pick(h, hot):
    acc = jnp.zeros((512, 128), F32)
    for k in range(4):
        hk = pltpu.roll(h, 32 * k, 1) if k else h
        hi = hk.astype(BF16)
        mid = (hk - hi.astype(F32)).astype(BF16)
        both = jnp.dot(hot[k], jnp.concatenate([hi, mid], axis=1), preferred_element_type=F32)
        acc = acc + (both[:, :128] + both[:, 128:])
    return acc


def early_answer_kernel(hot, h0, h1, h2, out):
    h = h0[...] + pltpu.roll(h1[...], 6, 1) + pltpu.roll(h2[...], 12, 1)
    out[...] = pick(h, hot)


def answer_kernel(hot, early, h3, out):
    out[...] = (early[...] + pick(pltpu.roll(h3[...], 18, 1), hot)).reshape(128, 4, 128)


def building_start_kernel(d_in, v_in, hf, br, st, ms, yd, cnt, disp, vel, hyst, stiff, yld, gain):
    level = lax.broadcasted_iota(jnp.int32, (64, 128), 0)
    mask = jnp.where(level < cnt[0], 1.0, 0.0)
    y = yd[...] * mask
    stiff[...] = st[...] * mask
    yld[...] = y
    gain[...] = DT / ms[...]
    for c in range(3):
        disp[c] = d_in[c] * mask
        vel[c] = v_in[c] * mask
        flag = br[c]
        hyst[c] = jnp.where(flag == 1, y, jnp.where(flag == 2, -y, hf[c] * y))


def building_kernel(ret, key, kmod, cnt, d_in, v_in, h_in, st, yd, gn, d_out, v_out, h_out, ground, bufs, sem):
    pieces = split3(ret[...].reshape(512, 128).T)[:2]
    row512 = lax.broadcasted_iota(jnp.int32, (512, 128), 0).astype(F32)
    for j in range(8):
        lanes = pl.ds(128 * j, 128)
        hot = jnp.where(row512 == key[j : j + 1, :], 1.0, 0.0).astype(BF16)
        g = jnp.dot(pieces[0], hot, preferred_element_type=F32)
        g = g + jnp.dot(pieces[1], hot, preferred_element_type=F32)
        km = kmod[j : j + 1, :]
        acc = jnp.zeros((32, 128), F32)
        for k in range(4):
            acc = acc + jnp.where(km == k, g[32 * k : 32 * k + 32], 0.0)
        ground[:, lanes] = acc * (1.0 / DT)
    outs = (d_out, v_out, h_out)
    copies = []
    for c in range(3):

        def chunk(j, carry, c=c):
            lanes = pl.ds(pl.multiple_of(j * 128, 128), 128)
            level = lax.broadcasted_iota(jnp.int32, (64, 128), 0)
            first_row = level == 0
            last_row = level == 63
            mask = jnp.where(level < cnt[0:1, lanes], 1.0, 0.0)

            def drift_of(x):
                return x - jnp.where(first_row, 0.0, pltpu.roll(x, 1, 0))

            stiff = st[:, lanes]
            yld = yd[:, lanes]
            gain = gn[:, lanes]
            disp = d_in[c, :, lanes]
            vel = v_in[c, :, lanes]
            hyst = h_in[c, :, lanes]
            drift = drift_of(disp)
            for t in range(STEPS):
                spring = stiff * (POST * drift + (1.0 - POST) * hyst)
                above = jnp.where(last_row, 0.0, pltpu.roll(spring, 63, 0))
                row = ground[3 * t + c : 3 * t + c + 1, lanes]
                vel = vel * (1.0 - DT * DAMP) + (gain * (above - spring) - mask * row)
                disp = disp + DT * vel
                new = drift_of(disp)
                hyst = jnp.minimum(jnp.maximum(hyst + new - drift, -yld), yld)
                drift = new
            bufs[0, c, :, lanes] = disp
            bufs[1, c, :, lanes] = vel
            bufs[2, c, :, lanes] = hyst
            return carry

        lax.fori_loop(0, 8, chunk, 0)
        for n in range(3):
            cp = pltpu.make_async_copy(bufs.at[n, c], outs[n].at[c], sem.at[3 * c + n])
            cp.start()
            copies.append(cp)
    for cp in copies:
        cp.wait()


def building_start(sd, sv, hf, br, st, ms, yd, cnt):
    lanes3 = pl.BlockSpec((3, 64, 128), lambda i: (0, 0, i))
    lanes2 = pl.BlockSpec((64, 128), lambda i: (0, i))
    rows = pl.BlockSpec((1, 1, 128), lambda i: (i, 0, 0))
    return pl.pallas_call(
        building_start_kernel,
        out_shape=[sds(3, 64, 1024)] * 3 + [sds(64, 1024)] * 3,
        grid=(8,),
        in_specs=[lanes3] * 4 + [lanes2] * 3 + [rows],
        out_specs=[lanes3] * 3 + [lanes2] * 3,
        compiler_params=CP,
        name="building_start",
    )(sd, sv, hf, br, st, ms, yd, cnt.reshape(8, 1, 128))


def local(u, p, de, mu, la, sd, sv, hf, br, st, ms, yd, cnt, tile, cell):
    ix = lax.axis_index("gx")
    iy = lax.axis_index("gy")
    nx = lax.axis_size("gx")
    ny = lax.axis_size("gy")
    edge = jnp.stack([ix > 0, ix < nx - 1, iy > 0, iy < ny - 1]).astype(F32).reshape(1, 4)

    hbm = [pltpu.with_memory_space_constraint(x, pltpu.HBM) for x in (u, p, la, mu, de)]
    up, down, right, left = pl.pallas_call(
        pack_first_kernel,
        out_shape=[sds(XPLANES, 32, 128)] * 2 + [sds(144, 8, 128)] * 2,
        in_specs=[HB] * 5,
        out_specs=[VM] * 4,
        scratch_shapes=[pltpu.SemaphoreType.DMA((36,))],
        compiler_params=CP,
        name="pack_first",
    )(*hbm)
    north, south = ring(up, "gx", 1), ring(down, "gx", -1)
    west, east = ring(right, "gy", 1), ring(left, "gy", -1)

    req, key, kmod = pl.pallas_call(
        request_kernel,
        out_shape=[sds(128, 4, 128), sds(8, 128), sds(8, 128)],
        in_specs=[VM] * 2,
        out_specs=[VM] * 3,
        scratch_shapes=[pltpu.VMEM((512, 1024), BF16), pltpu.VMEM((128, 1024), BF16), pltpu.VMEM((128, 1024), BF16)],
        compiler_params=CP,
        name="requests",
    )(tile.reshape(8, 128).astype(F32), cell.reshape(8, 128).astype(F32))
    incoming = lax.all_to_all(req, ("gx", "gy"), 0, 0, tiled=True)
    north, south, west, east, incoming = lax.optimization_barrier((north, south, west, east, incoming))

    def corners(north, south):
        n = north.shape[0]
        right, left = pl.pallas_call(
            pack_corner_kernel,
            out_shape=[sds(2, n, 8, 128)] * 2,
            in_specs=[VM] * 2,
            out_specs=[VM] * 2,
            compiler_params=CP,
            name="pack_corner",
        )(north, south)
        return ring(right, "gy", 1), ring(left, "gy", -1)

    half = sds(3, 8, 32, 128)
    side = sds(3, 16, 8, 128)
    band = pltpu.VMEM((256, 128), BF16)
    work = [sds(3, 32, YR, 128), sds(6, 28, YR, 128), sds(6, 20, YR, 128), sds(16, 48, 128), sds(3, 24, YR, 128), half, half, sds(512, 128)]
    mats = [sds(3, 24, YR, 128), sds(28, YR, 128), sds(28, YR, 128), sds(24, YR, 128)]
    wc, ec = corners(north, south)
    state = pl.pallas_call(
        first_round_kernel,
        out_shape=work + mats,
        in_specs=[SM] + [HB] * 5 + [VM] * 4,
        out_specs=[VM] * 12,
        scratch_shapes=[band, pltpu.SemaphoreType.DMA((9,))],
        compiler_params=CP,
        name="wave_first",
    )(edge, *hbm, north, south, west, east)
    state = pl.pallas_call(
        first_patch_kernel,
        out_shape=work + mats + [side, side],
        in_specs=[SM] + [VM] * 14,
        out_specs=[VM] * 14,
        input_output_aliases={3 + n: n for n in range(12)},
        scratch_shapes=[band],
        compiler_params=CP,
        name="patch_first",
    )(edge, wc, ec, *state)
    prev, top, bot, hist = state[4:8]
    lam, mu2, q = state[9:12]
    right, left = state[12:14]
    hists = [hist]
    for r in range(1, 4):
        north, south = ring(bot.reshape(24, 32, 128), "gx", 1), ring(top.reshape(24, 32, 128), "gx", -1)
        west, east = ring(right, "gy", 1), ring(left, "gy", -1)
        if r == 1:
            starts = building_start(sd, sv, hf, br, st, ms, yd, cnt)
            hot = pl.pallas_call(
                hot_kernel,
                out_shape=jax.ShapeDtypeStruct((4, 512, 512), BF16),
                in_specs=[VM],
                out_specs=VM,
                compiler_params=CP,
                name="hot",
            )(incoming)
            north, south, hot, starts = lax.optimization_barrier((north, south, hot, starts))
        if r == 3:
            early = pl.pallas_call(
                early_answer_kernel,
                out_shape=sds(512, 128),
                in_specs=[VM] * 4,
                out_specs=VM,
                compiler_params=CP,
                name="early_answers",
            )(hot, *hists)
            north, south, early = lax.optimization_barrier((north, south, early))
        wc, ec = corners(north, south)
        consts = (prev, lam, mu2, q)
        state = pl.pallas_call(
            round_kernel,
            out_shape=work,
            in_specs=[SM] + [VM] * 10,
            out_specs=[VM] * 8,
            scratch_shapes=[band],
            compiler_params=CP,
            name="wave_round",
        )(edge, top, bot, north, south, west, east, *consts)
        last = r == 3
        state = pl.pallas_call(
            last_patch_kernel if last else patch_kernel,
            out_shape=work + ([sds(3, 16, 32, 128)] * 2 if last else [side, side]),
            in_specs=[SM] + [VM] * 14,
            out_specs=[VM] * 10,
            input_output_aliases={7 + n: n for n in range(8)},
            scratch_shapes=([pltpu.VMEM((3, 16, 8, 128), F32)] * 2 if last else []) + [band],
            compiler_params=CP,
            name="patch_last" if last else "patch_round",
        )(edge, wc, ec, *consts, *state)
        prev, top, bot, hist, right, left = state[4:10]
        hists.append(hist)
    now, before = right, left

    answers = pl.pallas_call(
        answer_kernel,
        out_shape=sds(128, 4, 128),
        in_specs=[VM] * 3,
        out_specs=VM,
        compiler_params=CP,
        name="answers",
    )(hot, early, hists[3])
    returned = lax.all_to_all(answers, ("gx", "gy"), 0, 0, tiled=True)
    disp, vel, hyst = pl.pallas_call(
        building_kernel,
        out_shape=[sds(3, 64, 1024)] * 3,
        in_specs=[VM] * 10,
        out_specs=[HB] * 3,
        scratch_shapes=[
            pltpu.VMEM((32, 1024), F32),
            pltpu.VMEM((3, 3, 64, 1024), F32),
            pltpu.SemaphoreType.DMA((9,)),
        ],
        compiler_params=CP,
        name="buildings",
    )(returned, key, kmod, cnt.reshape(1, 1024), *starts)
    return now, before, disp, vel, hyst


def solution(mesh):
    grid = P(None, "gx", "gy", None)
    cells = P("gx", "gy", None)
    both = ("gx", "gy")
    b3 = P(None, None, both)
    b2 = P(None, both)
    b1 = P(both)
    return jax.shard_map(
        local,
        mesh=mesh,
        in_specs=(grid, grid, cells, cells, cells, b3, b3, b3, b3, b2, b2, b2, b1, P(both, None), b1),
        out_specs=(grid, grid, b3, b3, b3),
        check_vma=False,
    )
```

```python
import jax
import jax.numpy as jnp
from jax import lax
from jax.experimental import pallas as pl
from jax.experimental.pallas import tpu as pltpu
from jax.sharding import PartitionSpec as P

STEPS = 8
DT = 0.35
POST = 0.1
DAMP = 0.05
F32 = jnp.float32
BF16 = jnp.bfloat16
VM = pl.BlockSpec(memory_space=pltpu.VMEM)
SM = pl.BlockSpec(memory_space=pltpu.SMEM)
HB = pl.BlockSpec(memory_space=pltpu.HBM)
CP = pltpu.CompilerParams(vmem_limit_bytes=12 << 20)
BW = 128
YR = 56

XPARTS = ((0, 3, 8), (1, 3, 4), (2, 1, 6), (3, 1, 6), (4, 1, 4))
XPLANES = sum(c * w for _, c, w in XPARTS)


def sds(*shape):
    return jax.ShapeDtypeStruct(shape, F32)


def ring(x, axis, step):
    n = lax.axis_size(axis)
    return lax.ppermute(x, axis, [(i, (i + step) % n) for i in range(n)])


def split3(x):
    hi = x.astype(BF16)
    rest = x - hi.astype(F32)
    mid = rest.astype(BF16)
    low = (rest - mid.astype(F32)).astype(BF16)
    return hi, mid, low


def at_comp(ref, comps, c, rows, cols):
    return ref.at[c, rows, cols] if comps == 3 else ref.at[rows, cols]


def pack_first_kernel(u, p, la, mu, de, up, down, right, left, sem):
    args = (u, p, la, mu, de)
    copies = []
    off = 0
    row = 0
    for a, comps, w in XPARTS:
        for c in range(comps):
            full = pl.ds(0, 32)
            every = pl.ds(0, 16)
            for src, dst in (
                (at_comp(args[a], comps, c, pl.ds(16 - w, w), full), up.at[pl.ds(off, w)]),
                (at_comp(args[a], comps, c, pl.ds(0, w), full), down.at[pl.ds(off, w)]),
                (at_comp(args[a], comps, c, every, pl.ds(24, 8)), right.at[pl.ds(row, 16)]),
                (at_comp(args[a], comps, c, every, pl.ds(0, 8)), left.at[pl.ds(row, 16)]),
            ):
                cp = pltpu.make_async_copy(src, dst, sem.at[len(copies)])
                cp.start()
                copies.append(cp)
            off += w
            row += 16
    for cp in copies:
        cp.wait()


def pack_corner_kernel(north, south, right, left):
    for dst, col in ((right, 24), (left, 0)):
        dst[0] = north[:, col : col + 8]
        dst[1] = south[:, col : col + 8]


def z_matrix():
    i = lax.broadcasted_iota(jnp.int32, (256, 128), 0)
    j = lax.broadcasted_iota(jnp.int32, (256, 128), 1)
    d = jnp.where(i < 128, i, i - 128) - j
    one = jnp.ones((256, 128), F32)
    near = jnp.where(d == 1, 8.0 * one, 0.0) - jnp.where(d == -1, 8.0 * one, 0.0)
    far = jnp.where(d == 2, one, 0.0) - jnp.where(d == -2, one, 0.0)
    return (near - far).astype(BF16)


def pieces2(f):
    hi = f.astype(BF16)
    lo = (f - hi.astype(F32)).astype(BF16)
    return jnp.concatenate([hi, lo], axis=1)


def dz_all(fields, mz):
    n = fields[0].shape[0]
    lhs = pieces2(jnp.concatenate(fields, axis=0))
    out = jnp.dot(lhs, mz, preferred_element_type=F32)
    return [out[n * k : n * k + n] for k in range(len(fields))]


def dx(rows, k):
    return 8.0 * (rows[k + 3] - rows[k + 1]) - (rows[k + 4] - rows[k])


def dy(ref, c, x, y, n):
    near = ref[c, x, pl.ds(y + 1, n)] - ref[c, x, pl.ds(y - 1, n)]
    far = ref[c, x, pl.ds(y + 2, n)] - ref[c, x, pl.ds(y - 2, n)]
    return 8.0 * near - far


def for_x(count, fn):
    def body(i, carry):
        fn(i)
        return carry

    lax.fori_loop(0, count, body, 0)


def stress_rows(u, ux, s, sx, lam, mu, mz, blocks, m, n):
    rows = []
    fields = []
    for g0, y in blocks:
        r = [[u[c, g0 - ux - 2 + j, pl.ds(y, n)] for j in range(m + 4)] for c in range(3)]
        rows.append(r)
        fields += [r[c][k + 2] for k in range(m) for c in range(3)]
    zs = dz_all(fields, mz[...])
    for (g0, y), r in zip(blocks, rows):
        ys = pl.ds(y, n)
        for k in range(m):
            gx = g0 + k
            x = gx - ux
            z0, z1, z2 = zs[:3]
            zs = zs[3:]
            mm = mu[gx - 2, ys]
            g00 = dx(r[0], k)
            g11 = dy(u, 1, x, y, n)
            lt = lam[gx - 2, ys] * (g00 + g11 + z2)
            m2 = mm + mm
            s[0, gx - sx, ys] = lt + m2 * g00
            s[1, gx - sx, ys] = lt + m2 * g11
            s[2, gx - sx, ys] = lt + m2 * z2
            s[3, gx - sx, ys] = mm * (dy(u, 0, x, y, n) + dx(r[1], k))
            s[4, gx - sx, ys] = mm * (z0 + dx(r[2], k))
            s[5, gx - sx, ys] = mm * (z1 + dy(u, 2, x, y, n))


def forces(s, sx, q, mz, blocks, m, n):
    rows = []
    fields = []
    for g0, y in blocks:
        ys = pl.ds(y, n)
        r = [[s[c, g0 - sx - 2 + j, ys] for j in range(m + 4)] for c in (0, 3, 4)]
        rows.append(r)
        for k in range(m):
            fields += [r[2][k + 2], s[5, g0 - sx + k, ys], s[2, g0 - sx + k, ys]]
    zs = dz_all(fields, mz[...])
    out = []
    for (g0, y), r in zip(blocks, rows):
        mine = []
        for k in range(m):
            x = g0 + k
            z0, z1, z2 = zs[:3]
            zs = zs[3:]
            qk = q[x - 4, pl.ds(y, n)]
            mine.append(
                (
                    qk * (dx(r[0], k) + dy(s, 3, x - sx, y, n) + z0),
                    qk * (dx(r[1], k) + dy(s, 1, x - sx, y, n) + z1),
                    qk * (dx(r[2], k) + dy(s, 5, x - sx, y, n) + z2),
                )
            )
        out.append(mine)
    return out


def surface(fs, slot, old):
    lane = lax.broadcasted_iota(jnp.int32, fs[0].shape, 1)
    for c, f in enumerate(fs):
        v = pltpu.roll(f, slot + c, 1) if slot + c else f
        old = jnp.where(lane == slot + c, v, old)
    return old


def first_rows(ue, prev, q, s, hs, mz, u1, blocks, m, n, seen):
    for (i0, y), fr in zip(blocks, forces(s, 2, q, mz, [(i0 + 4, y) for i0, y in blocks], m, n)):
        ys = pl.ds(y, n)
        for k, fs in enumerate(fr):
            i = i0 + k
            if k in seen(i0):
                hs[i - 4, pl.ds(y - 4, n)] = surface(fs, 0, jnp.zeros((n, 128), F32))
            for c in range(3):
                now = ue[c, i + 4, ys]
                u1[c, i, ys] = (now - prev[c, i, ys]) + (now + fs[c])


def second_rows(ue, q, s, hs, mz, u1, hist, blocks, m, n):
    places = [(j0 + 8 * part + 8, y) for _, j0, part, y, _ in blocks]
    for (out, j0, part, y, side), fr in zip(blocks, forces(s, 6, q, mz, places, m, n)):
        ys = pl.ds(y, n)
        for k, fs in enumerate(fr):
            i = j0 + 8 * part + k
            r = i * 32 + y - 8
            hist[pl.ds(r, n)] = surface(fs, 3, hs[i, pl.ds(y - 4, n)])
            for c in range(3):
                now = u1[c, i + 4, ys]
                v = (now - ue[c, i + 8, ys]) + (now + fs[c])
                out[c, j0 + k, pl.ds(y - 8, n)] = v
                if side is not None:
                    side[c, i] = v


def two_steps(prev, lam, mu, q, ue, s, s2, hs, u1, top, bot, hist, mz):
    mz[...] = z_matrix()
    none = lambda i0: ()
    every = lambda i0: range(8)
    for_x(2, lambda i: stress_rows(ue, 0, s, 2, lam, mu, mz, [(14 * i + 2, 2)], 14, 48))
    first_rows(ue, prev, q, s, hs, mz, u1, [(0, 4), (20, 4)], 4, 48, none)
    for_x(2, lambda i: first_rows(ue, prev, q, s, hs, mz, u1, [(8 * i + 4, 4)], 8, 48, every))
    for_x(2, lambda i: stress_rows(u1, 4, s2, 6, lam, mu, mz, [(10 * i + 6, 6)], 10, 48))
    for part, out in enumerate((top, bot)):
        second_rows(ue, q, s2, hs, mz, u1, hist, [(out, 0, part, 8, None)], 8, 32)


def patch_two_steps(prev, lam, mu, q, ue, s, s2, hs, u1, top, bot, hist, right, left, mz):
    mz[...] = z_matrix()
    stress_rows(ue, 0, s, 2, lam, mu, mz, [(x, y) for x in (2, 22) for y in (2, 38)], 8, 8)
    seen = lambda i0: range(4, 8) if i0 == 0 else range(4)
    first_rows(ue, prev, q, s, hs, mz, u1, [(i, y) for i in (0, 16) for y in (4, 36)], 8, 8, seen)
    stress_rows(u1, 4, s2, 6, lam, mu, mz, [(x, y) for x in (6, 18) for y in (6, 34)], 8, 8)
    blocks = [(o, 0, part, y, side) for part, o in enumerate((top, bot)) for y, side in ((8, left), (32, right))]
    second_rows(ue, q, s2, hs, mz, u1, hist, blocks, 8, 8)


def first_round_kernel(flags, u, p, la, mu, de, north, south, west, east, ue, s, s2, hs, u1, top, bot, hist, pe, lam, muo, q, mz, sem):
    fn, fs, fw, fe = [flags[0, k] for k in range(4)]
    copies = []
    args = (u, p, la, mu, de)
    exts = (ue, pe, lam, muo, q)
    off = 0
    row = 0
    for a, comps, w in XPARTS:
        for c in range(comps):
            ref = exts[a].at[c] if comps == 3 else exts[a]
            arg = args[a].at[c] if comps == 3 else args[a]
            cp = pltpu.make_async_copy(arg, ref.at[pl.ds(w, 16), pl.ds(8, 32)], sem.at[len(copies)])
            cp.start()
            copies.append(cp)
            none = jnp.zeros((8, 128), F32)
            for i in range(w):
                for x, strip, f in ((i, north, fn), (16 + w + i, south, fs)):
                    ref[x, 0:8] = none
                    ref[x, 8:40] = strip[off + i] * f
                    ref[x, 40:48] = none

            def mid(i, ref=ref, row=row, w=w):
                ref[w + i, 0:8] = west[row + i] * fw
                ref[w + i, 40:48] = east[row + i] * fe

            for_x(16, mid)
            off += w
            row += 16

    for cp in copies:
        cp.wait()

    def scale(i):
        lam[i, 0:48] = lam[i, 0:48] * (1.0 / 12.0)
        muo[i, 0:48] = muo[i, 0:48] * (1.0 / 12.0)

    for_x(28, scale)

    def invert(i):
        q[i, 0:48] = inverse_density(q[i, 0:48])

    for_x(24, invert)
    two_steps(pe, lam, muo, q, ue, s, s2, hs, u1, top, bot, hist, mz)


def inverse_density(d):
    return jnp.where(d > 0.0, (DT * DT / 12.0) / jnp.where(d > 0.0, d, 1.0), 0.0)


def first_patch_kernel(*refs):
    flags, wc, ec = refs[:3]
    ue, s, s2, hs, u1, top, bot, hist, pe, lam, mu, q, right, left, mz = refs[15:]
    fn, fs, fw, fe = [flags[0, k] for k in range(4)]
    exts = (ue, pe, lam, mu, q)
    off = 0
    for a, comps, w in XPARTS:
        for c in range(comps):
            ref = exts[a].at[c] if comps == 3 else exts[a]
            for i in range(w):
                for half, x, f in ((0, i, fn), (1, 16 + w + i, fs)):
                    for strip, y, g in ((wc, 0, fw), (ec, 40, fe)):
                        v = strip[half, off + i] * (f * g)
                        if a in (2, 3):
                            v = v * (1.0 / 12.0)
                        ref[x, y : y + 8] = inverse_density(v) if a == 4 else v
            off += w
    patch_two_steps(pe, lam, mu, q, ue, s, s2, hs, u1, top, bot, hist, right, left, mz)


def round_kernel(flags, top, bot, north, south, west, east, prev, lam, mu, q, ue, s, s2, hs, u1, top2, bot2, hist, mz):
    fn, fs, fw, fe = [flags[0, k] for k in range(4)]
    none = jnp.zeros((8, 128), F32)
    for c in range(3):

        def rows(i, c=c):
            for x, strip, f in ((i, north, fn), (24 + i, south, fs)):
                ue[c, x, 0:8] = none
                ue[c, x, 8:40] = strip[8 * c + i] * f
                ue[c, x, 40:48] = none
            for x, strip in ((i, top), (8 + i, bot)):
                ue[c, 8 + x, 0:8] = west[c, x] * fw
                ue[c, 8 + x, 8:40] = strip[c, i]
                ue[c, 8 + x, 40:48] = east[c, x] * fe

        for_x(8, rows)
    two_steps(prev, lam, mu, q, ue, s, s2, hs, u1, top2, bot2, hist, mz)


def fill_corners(flags, wc, ec, ue):
    fn, fs, fw, fe = [flags[0, k] for k in range(4)]
    for c in range(3):

        def rows(i, c=c):
            for half, x, f in ((0, i, fn), (1, 24 + i, fs)):
                ue[c, x, 0:8] = wc[half, 8 * c + i] * (f * fw)
                ue[c, x, 40:48] = ec[half, 8 * c + i] * (f * fe)

        for_x(8, rows)


def patch_kernel(*refs):
    flags, wc, ec, prev, lam, mu, q = refs[:7]
    ue, s, s2, hs, u1, top, bot, hist, right, left, mz = refs[15:]
    fill_corners(flags, wc, ec, ue)
    patch_two_steps(prev, lam, mu, q, ue, s, s2, hs, u1, top, bot, hist, right, left, mz)


def request_kernel(tile, cell, req, key, kmod, a_ref, bhi, blo):
    ones = jnp.ones((128, 128), F32)
    sub = lax.broadcasted_iota(jnp.int32, (128, 128), 0)
    lan = lax.broadcasted_iota(jnp.int32, (128, 128), 1)
    cols = [(ones * tile[i : i + 1, :]).T for i in range(8)]
    row512 = lax.broadcasted_iota(jnp.int32, (512, 128), 0).astype(F32)
    subf = sub.astype(F32)
    for j in range(8):
        mine = tile[j : j + 1, :]
        acc = jnp.where((cols[j] == mine) & (sub < lan), 1.0, 0.0)
        for i in range(j):
            acc = acc + jnp.where(cols[i] == mine, 1.0, 0.0)
        rank = jnp.sum(acc, axis=0, keepdims=True)
        quarter = jnp.floor(rank * 0.25)
        kj = mine * 4.0 + quarter
        mj = rank - 4.0 * quarter
        key[j : j + 1, :] = kj
        kmod[j : j + 1, :] = mj
        lanes = pl.ds(128 * j, 128)
        a_ref[:, lanes] = jnp.where(row512 == kj, 1.0, 0.0).astype(BF16)
        cj = cell[j : j + 1, :]
        hi = jnp.floor(cj * (1.0 / 32.0))
        hit = subf == mj
        bhi[:, lanes] = jnp.where(hit, hi, 0.0).astype(BF16)
        blo[:, lanes] = jnp.where(hit, cj - 32.0 * hi, 0.0).astype(BF16)
    dims = (((1,), (1,)), ((), ()))
    top = lax.dot_general(a_ref[...], bhi[...], dims, preferred_element_type=F32)
    low = lax.dot_general(a_ref[...], blo[...], dims, preferred_element_type=F32)
    req[...] = (32.0 * top + low).reshape(128, 4, 128)


def hot_kernel(inc, hot):
    cells = inc[...].reshape(512, 128)
    lane = lax.broadcasted_iota(jnp.int32, (512, 512), 1).astype(F32)
    for k in range(4):
        hot[k] = jnp.where(lane == cells[:, k : k + 1], 1.0, 0.0).astype(BF16)


def pick(h, hot):
    acc = jnp.zeros((512, 128), F32)
    for k in range(4):
        hk = pltpu.roll(h, 32 * k, 1) if k else h
        hi = hk.astype(BF16)
        mid = (hk - hi.astype(F32)).astype(BF16)
        both = jnp.dot(hot[k], jnp.concatenate([hi, mid], axis=1), preferred_element_type=F32)
        acc = acc + (both[:, :128] + both[:, 128:])
    return acc


def early_answer_kernel(hot, h0, h1, h2, key, out, hots):
    row512 = lax.broadcasted_iota(jnp.int32, (512, 128), 0).astype(F32)
    for j in range(8):
        hots[:, 128 * j : 128 * j + 128] = jnp.where(row512 == key[j : j + 1, :], 1.0, 0.0).astype(BF16)
    h = h0[...] + pltpu.roll(h1[...], 6, 1) + pltpu.roll(h2[...], 12, 1)
    out[...] = pick(h, hot)


def answer_kernel(hot, early, h3, out):
    out[...] = (early[...] + pick(pltpu.roll(h3[...], 18, 1), hot)).reshape(128, 4, 128)


def building_start_kernel(d_in, v_in, hf, br, st, ms, yd, cnt, disp, vel, hyst, weak, stiff, yld, gain):
    low = lax.broadcasted_iota(jnp.int32, (8, 128), 0) * 8
    for v in range(8):
        src = pl.ds(v, 8, stride=8)
        dst = pl.ds(8 * v, 8)
        mask = jnp.where(low + v < cnt[0], 1.0, 0.0)
        y = yd[src] * mask
        k = st[src] * mask
        weak[dst] = POST * k
        stiff[dst] = (1.0 - POST) * k
        yld[dst] = y
        gain[dst] = DT * DT / ms[src]
        for c in range(3):
            disp[c, dst] = d_in[c, src] * mask
            vel[c, dst] = v_in[c, src] * (DT * mask)
            flag = br[c, src]
            hyst[c, dst] = jnp.where(flag == 1, y, jnp.where(flag == 2, -y, hf[c, src] * y))


def building_kernel(*refs):
    top, bot, u1, ret, hots, kmod, cnt, d_in, v_in, h_in, wk, st, yd, gn = refs[:14]
    now, before, d_out, v_out, h_out, ground, bufs, sem, field_sem = refs[14:]
    copies = []
    for n, (src, dst) in enumerate(
        (
            (top, now.at[pl.ds(0, 3), pl.ds(0, 8)]),
            (bot, now.at[pl.ds(0, 3), pl.ds(8, 8)]),
            (u1.at[pl.ds(0, 3), pl.ds(4, 16), pl.ds(8, 32)], before),
        )
    ):
        cp = pltpu.make_async_copy(src, dst, field_sem.at[n])
        cp.start()
        copies.append(cp)
    turned = ret[...].reshape(512, 128).T
    high = turned.astype(BF16)
    low = (turned - high.astype(F32)).astype(BF16)
    both = jnp.dot(jnp.concatenate([high, low], axis=0), hots[...], preferred_element_type=F32)
    gathered = both[:128] + both[128:]
    for j in range(8):
        g = gathered[:, 128 * j : 128 * j + 128]
        km = kmod[j : j + 1, :]
        acc = jnp.zeros((32, 128), F32)
        for k in range(4):
            acc = acc + jnp.where(km == k, g[32 * k : 32 * k + 32], 0.0)
        ground[:, 128 * j : 128 * j + 128] = acc
    outs = (d_out, v_out, h_out)
    eight = range(8)
    for c in range(3):

        def chunk(j, c=c):
            lanes = pl.ds(pl.multiple_of(j * BW, BW), BW)
            row = lax.broadcasted_iota(jnp.int32, (8, BW), 0)
            first_row = row == 0
            last_row = row == 7
            count = cnt[0:1, lanes]
            part = [pl.ds(8 * v, 8) for v in eight]

            def drift_of(x):
                below = jnp.where(first_row, 0.0, pltpu.roll(x[7], 1, 0))
                return [x[0] - below] + [x[v] - x[v - 1] for v in range(1, 8)]

            mask = [jnp.where(row * 8 + v < count, 1.0, 0.0) for v in eight]
            disp = [d_in[c, part[v], lanes] for v in eight]
            vel = [v_in[c, part[v], lanes] for v in eight]
            hyst = [h_in[c, part[v], lanes] for v in eight]
            drift = drift_of(disp)
            for t in range(STEPS):
                spring = [wk[part[v], lanes] * drift[v] + st[part[v], lanes] * hyst[v] for v in eight]
                above = spring[1:] + [jnp.where(last_row, 0.0, pltpu.roll(spring[0], 7, 0))]
                quake = ground[3 * t + c : 3 * t + c + 1, lanes]
                for v in eight:
                    push = gn[part[v], lanes] * (above[v] - spring[v]) - mask[v] * quake
                    vel[v] = vel[v] * (1.0 - DT * DAMP) + push
                    disp[v] = disp[v] + vel[v]
                new = drift_of(disp)
                for v in eight:
                    y = yd[part[v], lanes]
                    hyst[v] = jnp.minimum(jnp.maximum(hyst[v] + (new[v] - drift[v]), -y), y)
                drift = new
            for v in eight:
                dst = pl.ds(v, 8, stride=8)
                speed = vel[v] * (1.0 / DT)
                for h in range(BW // 128):
                    cut = slice(128 * h, 128 * h + 128)
                    bufs[0, c, j * (BW // 128) + h, dst] = disp[v][:, cut]
                    bufs[1, c, j * (BW // 128) + h, dst] = speed[:, cut]
                    bufs[2, c, j * (BW // 128) + h, dst] = hyst[v][:, cut]

        for_x(1024 // BW, chunk)
        for n in range(3):
            for j in range(8):
                dst = outs[n].at[c, pl.ds(0, 64), pl.ds(128 * j, 128)]
                cp = pltpu.make_async_copy(bufs.at[n, c, j], dst, sem.at[24 * c + 8 * n + j])
                cp.start()
                copies.append(cp)
    for cp in copies:
        cp.wait()


def building_start(sd, sv, hf, br, st, ms, yd, cnt):
    lanes3 = pl.BlockSpec((3, 64, 128), lambda i: (0, 0, i))
    lanes2 = pl.BlockSpec((64, 128), lambda i: (0, i))
    rows = pl.BlockSpec((1, 1, 128), lambda i: (i, 0, 0))
    return pl.pallas_call(
        building_start_kernel,
        out_shape=[sds(3, 64, 1024)] * 3 + [sds(64, 1024)] * 4,
        grid=(8,),
        in_specs=[lanes3] * 4 + [lanes2] * 3 + [rows],
        out_specs=[lanes3] * 3 + [lanes2] * 4,
        compiler_params=CP,
        name="building_start",
    )(sd, sv, hf, br, st, ms, yd, cnt.reshape(8, 1, 128))


def local(u, p, de, mu, la, sd, sv, hf, br, st, ms, yd, cnt, tile, cell):
    ix = lax.axis_index("gx")
    iy = lax.axis_index("gy")
    nx = lax.axis_size("gx")
    ny = lax.axis_size("gy")
    edge = jnp.stack([ix > 0, ix < nx - 1, iy > 0, iy < ny - 1]).astype(F32).reshape(1, 4)

    half = sds(3, 8, 32, 128)
    side = sds(3, 16, 8, 128)
    band = pltpu.VMEM((256, 128), BF16)
    work = [sds(3, 32, YR, 128), sds(6, 28, YR, 128), sds(6, 20, YR, 128), sds(16, 48, 128), sds(3, 24, YR, 128), half, half, sds(512, 128)]
    mats = [sds(3, 24, YR, 128), sds(28, YR, 128), sds(28, YR, 128), sds(24, YR, 128)]
    hbm = [pltpu.with_memory_space_constraint(x, pltpu.HBM) for x in (u, p, la, mu, de)]
    up, down, right, left = pl.pallas_call(
        pack_first_kernel,
        out_shape=[sds(XPLANES, 32, 128)] * 2 + [sds(144, 8, 128)] * 2,
        in_specs=[HB] * 5,
        out_specs=[VM] * 4,
        scratch_shapes=[pltpu.SemaphoreType.DMA((36,))],
        compiler_params=CP,
        name="pack_first",
    )(*hbm)
    north, south = ring(up, "gx", 1), ring(down, "gx", -1)
    west, east = ring(right, "gy", 1), ring(left, "gy", -1)

    req, key, kmod = pl.pallas_call(
        request_kernel,
        out_shape=[sds(128, 4, 128), sds(8, 128), sds(8, 128)],
        in_specs=[VM] * 2,
        out_specs=[VM] * 3,
        scratch_shapes=[pltpu.VMEM((512, 1024), BF16)] + [pltpu.VMEM((128, 1024), BF16)] * 2,
        compiler_params=CP,
        name="requests",
    )(tile.reshape(8, 128).astype(F32), cell.reshape(8, 128).astype(F32))
    incoming = lax.all_to_all(req, ("gx", "gy"), 0, 0, tiled=True)
    north, south, west, east, incoming = lax.optimization_barrier((north, south, west, east, incoming))

    def corners(north, south):
        n = north.shape[0]
        right, left = pl.pallas_call(
            pack_corner_kernel,
            out_shape=[sds(2, n, 8, 128)] * 2,
            in_specs=[VM] * 2,
            out_specs=[VM] * 2,
            compiler_params=CP,
            name="pack_corner",
        )(north, south)
        return ring(right, "gy", 1), ring(left, "gy", -1)

    wc, ec = corners(north, south)
    state = pl.pallas_call(
        first_round_kernel,
        out_shape=work + mats,
        in_specs=[SM] + [HB] * 5 + [VM] * 4,
        out_specs=[VM] * 12,
        scratch_shapes=[band, pltpu.SemaphoreType.DMA((9,))],
        compiler_params=CP,
        name="wave_first",
    )(edge, *hbm, north, south, west, east)
    state = pl.pallas_call(
        first_patch_kernel,
        out_shape=work + mats + [side, side],
        in_specs=[SM] + [VM] * 14,
        out_specs=[VM] * 14,
        input_output_aliases={3 + n: n for n in range(12)},
        scratch_shapes=[band],
        compiler_params=CP,
        name="patch_first",
    )(edge, wc, ec, *state)
    prev, top, bot, hist = state[4:8]
    lam, mu2, q = state[9:12]
    right, left = state[12:14]
    hists = [hist]
    for r in range(1, 4):
        north, south = ring(bot.reshape(24, 32, 128), "gx", 1), ring(top.reshape(24, 32, 128), "gx", -1)
        west, east = ring(right, "gy", 1), ring(left, "gy", -1)
        if r == 1:
            starts = building_start(sd, sv, hf, br, st, ms, yd, cnt)
            hot = pl.pallas_call(
                hot_kernel,
                out_shape=jax.ShapeDtypeStruct((4, 512, 512), BF16),
                in_specs=[VM],
                out_specs=VM,
                compiler_params=CP,
                name="hot",
            )(incoming)
            north, south, hot, starts = lax.optimization_barrier((north, south, hot, starts))
        if r == 3:
            early, hots = pl.pallas_call(
                early_answer_kernel,
                out_shape=[sds(512, 128), jax.ShapeDtypeStruct((512, 1024), BF16)],
                in_specs=[VM] * 5,
                out_specs=[VM] * 2,
                compiler_params=CP,
                name="early_answers",
            )(hot, *hists, key)
            north, south, early, hots = lax.optimization_barrier((north, south, early, hots))
        wc, ec = corners(north, south)
        consts = (prev, lam, mu2, q)
        state = pl.pallas_call(
            round_kernel,
            out_shape=work,
            in_specs=[SM] + [VM] * 10,
            out_specs=[VM] * 8,
            scratch_shapes=[band],
            compiler_params=CP,
            name="wave_round",
        )(edge, top, bot, north, south, west, east, *consts)
        state = pl.pallas_call(
            patch_kernel,
            out_shape=work + [side, side],
            in_specs=[SM] + [VM] * 14,
            out_specs=[VM] * 10,
            input_output_aliases={7 + n: n for n in range(8)},
            scratch_shapes=[band],
            compiler_params=CP,
            name="patch_round",
        )(edge, wc, ec, *consts, *state)
        prev, top, bot, hist, right, left = state[4:10]
        hists.append(hist)

    answers = pl.pallas_call(
        answer_kernel,
        out_shape=sds(128, 4, 128),
        in_specs=[VM] * 3,
        out_specs=VM,
        compiler_params=CP,
        name="answers",
    )(hot, early, hists[3])
    returned = lax.all_to_all(answers, ("gx", "gy"), 0, 0, tiled=True)
    now, before, disp, vel, hyst = pl.pallas_call(
        building_kernel,
        out_shape=[sds(3, 16, 32, 128)] * 2 + [sds(3, 64, 1024)] * 3,
        in_specs=[VM] * 14,
        out_specs=[HB] * 5,
        scratch_shapes=[
            pltpu.VMEM((32, 1024), F32),
            pltpu.VMEM((3, 3, 8, 64, 128), F32),
            pltpu.SemaphoreType.DMA((72,)),
            pltpu.SemaphoreType.DMA((3,)),
        ],
        compiler_params=CP,
        name="buildings",
    )(top, bot, prev, returned, hots, kmod, cnt.reshape(1, 1024), *starts)
    return now, before, disp, vel, hyst


def solution(mesh):
    grid = P(None, "gx", "gy", None)
    cells = P("gx", "gy", None)
    both = ("gx", "gy")
    b3 = P(None, None, both)
    b2 = P(None, both)
    b1 = P(both)
    return jax.shard_map(
        local,
        mesh=mesh,
        in_specs=(grid, grid, cells, cells, cells, b3, b3, b3, b3, b2, b2, b2, b1, P(both, None), b1),
        out_specs=(grid, grid, b3, b3, b3),
        check_vma=False,
    )
```

```python
import jax
import jax.numpy as jnp
from jax import lax
from jax.experimental import pallas as pl
from jax.experimental.pallas import tpu as pltpu
from jax.sharding import PartitionSpec as P

STEPS = 8
DT = 0.35
POST = 0.1
DAMP = 0.05
F32 = jnp.float32
BF16 = jnp.bfloat16
VM = pl.BlockSpec(memory_space=pltpu.VMEM)
SM = pl.BlockSpec(memory_space=pltpu.SMEM)
HB = pl.BlockSpec(memory_space=pltpu.HBM)
CP = pltpu.CompilerParams(vmem_limit_bytes=12 << 20)
BW = 128
YR = 56

XPARTS = ((0, 3, 8), (1, 3, 4), (2, 1, 6), (3, 1, 6), (4, 1, 4))
XPLANES = sum(c * w for _, c, w in XPARTS)


def sds(*shape):
    return jax.ShapeDtypeStruct(shape, F32)


def ring(x, axis, step):
    n = lax.axis_size(axis)
    return lax.ppermute(x, axis, [(i, (i + step) % n) for i in range(n)])


def split3(x):
    hi = x.astype(BF16)
    rest = x - hi.astype(F32)
    mid = rest.astype(BF16)
    low = (rest - mid.astype(F32)).astype(BF16)
    return hi, mid, low


def at_comp(ref, comps, c, rows, cols):
    return ref.at[c, rows, cols] if comps == 3 else ref.at[rows, cols]


def pack_first_kernel(u, p, la, mu, de, up, down, right, left, sem):
    args = (u, p, la, mu, de)
    copies = []
    off = 0
    row = 0
    for a, comps, w in XPARTS:
        for c in range(comps):
            full = pl.ds(0, 32)
            every = pl.ds(0, 16)
            for src, dst in (
                (at_comp(args[a], comps, c, pl.ds(16 - w, w), full), up.at[pl.ds(off, w)]),
                (at_comp(args[a], comps, c, pl.ds(0, w), full), down.at[pl.ds(off, w)]),
                (at_comp(args[a], comps, c, every, pl.ds(24, 8)), right.at[pl.ds(row, 16)]),
                (at_comp(args[a], comps, c, every, pl.ds(0, 8)), left.at[pl.ds(row, 16)]),
            ):
                cp = pltpu.make_async_copy(src, dst, sem.at[len(copies)])
                cp.start()
                copies.append(cp)
            off += w
            row += 16
    for cp in copies:
        cp.wait()


def pack_corner_kernel(north, south, right, left):
    for dst, col in ((right, 24), (left, 0)):
        dst[0] = north[:, col : col + 8]
        dst[1] = south[:, col : col + 8]


def z_matrix():
    i = lax.broadcasted_iota(jnp.int32, (256, 128), 0)
    j = lax.broadcasted_iota(jnp.int32, (256, 128), 1)
    d = jnp.where(i < 128, i, i - 128) - j
    one = jnp.ones((256, 128), F32)
    near = jnp.where(d == 1, 8.0 * one, 0.0) - jnp.where(d == -1, 8.0 * one, 0.0)
    far = jnp.where(d == 2, one, 0.0) - jnp.where(d == -2, one, 0.0)
    return (near - far).astype(BF16)


def pieces2(f):
    hi = f.astype(BF16)
    lo = (f - hi.astype(F32)).astype(BF16)
    return jnp.concatenate([hi, lo], axis=1)


def dz_all(fields, mz):
    n = fields[0].shape[0]
    lhs = pieces2(jnp.concatenate(fields, axis=0))
    out = jnp.dot(lhs, mz, preferred_element_type=F32)
    return [out[n * k : n * k + n] for k in range(len(fields))]


def dx(rows, k):
    return 8.0 * (rows[k + 3] - rows[k + 1]) - (rows[k + 4] - rows[k])


def dy(ref, c, x, y, n):
    near = ref[c, x, pl.ds(y + 1, n)] - ref[c, x, pl.ds(y - 1, n)]
    far = ref[c, x, pl.ds(y + 2, n)] - ref[c, x, pl.ds(y - 2, n)]
    return 8.0 * near - far


def for_x(count, fn):
    def body(i, carry):
        fn(i)
        return carry

    lax.fori_loop(0, count, body, 0)


def stress_rows(u, ux, s, sx, lam, mu, mz, blocks, m, n):
    rows = []
    fields = []
    for g0, y in blocks:
        r = [[u[c, g0 - ux - 2 + j, pl.ds(y, n)] for j in range(m + 4)] for c in range(3)]
        rows.append(r)
        fields += [r[c][k + 2] for k in range(m) for c in range(3)]
    zs = dz_all(fields, mz[...])
    for (g0, y), r in zip(blocks, rows):
        ys = pl.ds(y, n)
        for k in range(m):
            gx = g0 + k
            x = gx - ux
            z0, z1, z2 = zs[:3]
            zs = zs[3:]
            mm = mu[gx - 2, ys]
            g00 = dx(r[0], k)
            g11 = dy(u, 1, x, y, n)
            lt = lam[gx - 2, ys] * (g00 + g11 + z2)
            m2 = mm + mm
            s[0, gx - sx, ys] = lt + m2 * g00
            s[1, gx - sx, ys] = lt + m2 * g11
            s[2, gx - sx, ys] = lt + m2 * z2
            s[3, gx - sx, ys] = mm * (dy(u, 0, x, y, n) + dx(r[1], k))
            s[4, gx - sx, ys] = mm * (z0 + dx(r[2], k))
            s[5, gx - sx, ys] = mm * (z1 + dy(u, 2, x, y, n))


def forces(s, sx, q, mz, blocks, m, n):
    rows = []
    fields = []
    for g0, y in blocks:
        ys = pl.ds(y, n)
        r = [[s[c, g0 - sx - 2 + j, ys] for j in range(m + 4)] for c in (0, 3, 4)]
        rows.append(r)
        for k in range(m):
            fields += [r[2][k + 2], s[5, g0 - sx + k, ys], s[2, g0 - sx + k, ys]]
    zs = dz_all(fields, mz[...])
    out = []
    for (g0, y), r in zip(blocks, rows):
        mine = []
        for k in range(m):
            x = g0 + k
            z0, z1, z2 = zs[:3]
            zs = zs[3:]
            qk = q[x - 4, pl.ds(y, n)]
            mine.append(
                (
                    qk * (dx(r[0], k) + dy(s, 3, x - sx, y, n) + z0),
                    qk * (dx(r[1], k) + dy(s, 1, x - sx, y, n) + z1),
                    qk * (dx(r[2], k) + dy(s, 5, x - sx, y, n) + z2),
                )
            )
        out.append(mine)
    return out


def surface(fs, slot, old):
    lane = lax.broadcasted_iota(jnp.int32, fs[0].shape, 1)
    for c, f in enumerate(fs):
        v = pltpu.roll(f, slot + c, 1) if slot + c else f
        old = jnp.where(lane == slot + c, v, old)
    return old


def first_rows(ue, prev, q, s, hs, mz, u1, blocks, m, n, seen):
    for (i0, y), fr in zip(blocks, forces(s, 2, q, mz, [(i0 + 4, y) for i0, y in blocks], m, n)):
        ys = pl.ds(y, n)
        for k, fs in enumerate(fr):
            i = i0 + k
            if k in seen(i0):
                hs[i - 4, pl.ds(y - 4, n)] = surface(fs, 0, jnp.zeros((n, 128), F32))
            for c in range(3):
                now = ue[c, i + 4, ys]
                u1[c, i, ys] = (now - prev[c, i, ys]) + (now + fs[c])


def second_rows(ue, q, s, hs, mz, u1, hist, blocks, m, n):
    places = [(j0 + 8 * part + 8, y) for _, j0, part, y, _ in blocks]
    for (out, j0, part, y, side), fr in zip(blocks, forces(s, 6, q, mz, places, m, n)):
        ys = pl.ds(y, n)
        for k, fs in enumerate(fr):
            i = j0 + 8 * part + k
            r = i * 32 + y - 8
            hist[pl.ds(r, n)] = surface(fs, 3, hs[i, pl.ds(y - 4, n)])
            for c in range(3):
                now = u1[c, i + 4, ys]
                v = (now - ue[c, i + 8, ys]) + (now + fs[c])
                out[c, j0 + k, pl.ds(y - 8, n)] = v
                if side is not None:
                    side[c, i] = v


def two_steps(prev, lam, mu, q, ue, s, s2, hs, u1, top, bot, hist, mz):
    mz[...] = z_matrix()
    none = lambda i0: ()
    every = lambda i0: range(8)
    for_x(2, lambda i: stress_rows(ue, 0, s, 2, lam, mu, mz, [(14 * i + 2, 2)], 14, 48))
    first_rows(ue, prev, q, s, hs, mz, u1, [(0, 4), (20, 4)], 4, 48, none)
    for_x(2, lambda i: first_rows(ue, prev, q, s, hs, mz, u1, [(8 * i + 4, 4)], 8, 48, every))
    for_x(2, lambda i: stress_rows(u1, 4, s2, 6, lam, mu, mz, [(10 * i + 6, 6)], 10, 48))
    for part, out in enumerate((top, bot)):
        second_rows(ue, q, s2, hs, mz, u1, hist, [(out, 0, part, 8, None)], 8, 32)


def patch_two_steps(prev, lam, mu, q, ue, s, s2, hs, u1, top, bot, hist, right, left, mz):
    mz[...] = z_matrix()
    stress_rows(ue, 0, s, 2, lam, mu, mz, [(x, y) for x in (2, 22) for y in (2, 38)], 8, 8)
    seen = lambda i0: range(4, 8) if i0 == 0 else range(4)
    first_rows(ue, prev, q, s, hs, mz, u1, [(i, y) for i in (0, 16) for y in (4, 36)], 8, 8, seen)
    stress_rows(u1, 4, s2, 6, lam, mu, mz, [(x, y) for x in (6, 18) for y in (6, 34)], 8, 8)
    blocks = [(o, 0, part, y, side) for part, o in enumerate((top, bot)) for y, side in ((8, left), (32, right))]
    second_rows(ue, q, s2, hs, mz, u1, hist, blocks, 8, 8)


def first_round_kernel(flags, u, p, la, mu, de, north, south, west, east, ue, s, s2, hs, u1, top, bot, hist, pe, lam, muo, q, mz, sem):
    fn, fs, fw, fe = [flags[0, k] for k in range(4)]
    copies = []
    args = (u, p, la, mu, de)
    exts = (ue, pe, lam, muo, q)
    off = 0
    row = 0
    for a, comps, w in XPARTS:
        for c in range(comps):
            ref = exts[a].at[c] if comps == 3 else exts[a]
            arg = args[a].at[c] if comps == 3 else args[a]
            cp = pltpu.make_async_copy(arg, ref.at[pl.ds(w, 16), pl.ds(8, 32)], sem.at[len(copies)])
            cp.start()
            copies.append(cp)
            none = jnp.zeros((w, 8, 128), F32)
            for x, strip, f in ((0, north, fn), (16 + w, south, fs)):
                ref[x : x + w, 0:8] = none
                ref[x : x + w, 8:40] = strip[off : off + w] * f
                ref[x : x + w, 40:48] = none
            ref[w : w + 16, 0:8] = west[row : row + 16] * fw
            ref[w : w + 16, 40:48] = east[row : row + 16] * fe
            off += w
            row += 16
    for cp in copies:
        cp.wait()

    lam[:, 0:48] = lam[:, 0:48] * (1.0 / 12.0)
    muo[:, 0:48] = muo[:, 0:48] * (1.0 / 12.0)
    q[:, 0:48] = inverse_density(q[:, 0:48])
    two_steps(pe, lam, muo, q, ue, s, s2, hs, u1, top, bot, hist, mz)


def inverse_density(d):
    return jnp.where(d > 0.0, (DT * DT / 12.0) / jnp.where(d > 0.0, d, 1.0), 0.0)


def first_patch_kernel(*refs):
    flags, wc, ec = refs[:3]
    ue, s, s2, hs, u1, top, bot, hist, pe, lam, mu, q, right, left, mz = refs[15:]
    fn, fs, fw, fe = [flags[0, k] for k in range(4)]
    exts = (ue, pe, lam, mu, q)
    off = 0
    for a, comps, w in XPARTS:
        for c in range(comps):
            ref = exts[a].at[c] if comps == 3 else exts[a]
            for half, x, f in ((0, 0, fn), (1, 16 + w, fs)):
                for strip, y, g in ((wc, 0, fw), (ec, 40, fe)):
                    v = strip[half, off : off + w] * (f * g)
                    if a in (2, 3):
                        v = v * (1.0 / 12.0)
                    ref[x : x + w, y : y + 8] = inverse_density(v) if a == 4 else v
            off += w
    patch_two_steps(pe, lam, mu, q, ue, s, s2, hs, u1, top, bot, hist, right, left, mz)


def round_kernel(flags, top, bot, north, south, west, east, prev, lam, mu, q, ue, s, s2, hs, u1, top2, bot2, hist, mz):
    fn, fs, fw, fe = [flags[0, k] for k in range(4)]
    none = jnp.zeros((8, 8, 128), F32)
    for c in range(3):
        for x, strip, f in ((0, north, fn), (24, south, fs)):
            ue[c, x : x + 8, 0:8] = none
            ue[c, x : x + 8, 8:40] = strip[8 * c : 8 * c + 8] * f
            ue[c, x : x + 8, 40:48] = none
        ue[c, 8:24, 0:8] = west[c] * fw
        ue[c, 8:16, 8:40] = top[c]
        ue[c, 16:24, 8:40] = bot[c]
        ue[c, 8:24, 40:48] = east[c] * fe
    two_steps(prev, lam, mu, q, ue, s, s2, hs, u1, top2, bot2, hist, mz)


def fill_corners(flags, wc, ec, ue):
    fn, fs, fw, fe = [flags[0, k] for k in range(4)]
    for c in range(3):
        for half, x, f in ((0, 0, fn), (1, 24, fs)):
            ue[c, x : x + 8, 0:8] = wc[half, 8 * c : 8 * c + 8] * (f * fw)
            ue[c, x : x + 8, 40:48] = ec[half, 8 * c : 8 * c + 8] * (f * fe)


def patch_kernel(*refs):
    flags, wc, ec, prev, lam, mu, q = refs[:7]
    ue, s, s2, hs, u1, top, bot, hist, right, left, mz = refs[15:]
    fill_corners(flags, wc, ec, ue)
    patch_two_steps(prev, lam, mu, q, ue, s, s2, hs, u1, top, bot, hist, right, left, mz)


def request_kernel(tile, cell, req, key, kmod, a_ref, bhi, blo):
    ones = jnp.ones((128, 128), F32)
    sub = lax.broadcasted_iota(jnp.int32, (128, 128), 0)
    lan = lax.broadcasted_iota(jnp.int32, (128, 128), 1)
    cols = [(ones * tile[i : i + 1, :]).T for i in range(8)]
    row512 = lax.broadcasted_iota(jnp.int32, (512, 128), 0).astype(F32)
    subf = sub.astype(F32)
    for j in range(8):
        mine = tile[j : j + 1, :]
        acc = jnp.where((cols[j] == mine) & (sub < lan), 1.0, 0.0)
        for i in range(j):
            acc = acc + jnp.where(cols[i] == mine, 1.0, 0.0)
        rank = jnp.sum(acc, axis=0, keepdims=True)
        quarter = jnp.floor(rank * 0.25)
        kj = mine * 4.0 + quarter
        mj = rank - 4.0 * quarter
        key[j : j + 1, :] = kj
        kmod[j : j + 1, :] = mj
        lanes = pl.ds(128 * j, 128)
        a_ref[:, lanes] = jnp.where(row512 == kj, 1.0, 0.0).astype(BF16)
        cj = cell[j : j + 1, :]
        hi = jnp.floor(cj * (1.0 / 32.0))
        hit = subf == mj
        bhi[:, lanes] = jnp.where(hit, hi, 0.0).astype(BF16)
        blo[:, lanes] = jnp.where(hit, cj - 32.0 * hi, 0.0).astype(BF16)
    dims = (((1,), (1,)), ((), ()))
    top = lax.dot_general(a_ref[...], bhi[...], dims, preferred_element_type=F32)
    low = lax.dot_general(a_ref[...], blo[...], dims, preferred_element_type=F32)
    req[...] = (32.0 * top + low).reshape(128, 4, 128)


def hot_kernel(inc, hot):
    cells = inc[...].reshape(512, 128)
    lane = lax.broadcasted_iota(jnp.int32, (512, 512), 1).astype(F32)
    for k in range(4):
        hot[k] = jnp.where(lane == cells[:, k : k + 1], 1.0, 0.0).astype(BF16)


def pick(h, hot):
    acc = jnp.zeros((512, 128), F32)
    for k in range(4):
        hk = pltpu.roll(h, 32 * k, 1) if k else h
        hi = hk.astype(BF16)
        mid = (hk - hi.astype(F32)).astype(BF16)
        both = jnp.dot(hot[k], jnp.concatenate([hi, mid], axis=1), preferred_element_type=F32)
        acc = acc + (both[:, :128] + both[:, 128:])
    return acc


def early_answer_kernel(hot, h0, h1, h2, key, out, hots):
    row512 = lax.broadcasted_iota(jnp.int32, (512, 128), 0).astype(F32)
    for j in range(8):
        hots[:, 128 * j : 128 * j + 128] = jnp.where(row512 == key[j : j + 1, :], 1.0, 0.0).astype(BF16)
    h = h0[...] + pltpu.roll(h1[...], 6, 1) + pltpu.roll(h2[...], 12, 1)
    out[...] = pick(h, hot)


def answer_kernel(hot, early, h3, out):
    out[...] = (early[...] + pick(pltpu.roll(h3[...], 18, 1), hot)).reshape(128, 4, 128)


def building_start_kernel(d_in, v_in, hf, br, st, ms, yd, cnt, disp, vel, hyst, weak, stiff, yld, gain):
    low = lax.broadcasted_iota(jnp.int32, (8, 128), 0) * 8
    for v in range(8):
        src = pl.ds(v, 8, stride=8)
        dst = pl.ds(8 * v, 8)
        mask = jnp.where(low + v < cnt[0], 1.0, 0.0)
        y = yd[src] * mask
        k = st[src] * mask
        weak[dst] = POST * k
        stiff[dst] = (1.0 - POST) * k
        yld[dst] = y
        gain[dst] = DT * DT / ms[src]
        for c in range(3):
            disp[c, dst] = d_in[c, src] * mask
            vel[c, dst] = v_in[c, src] * (DT * mask)
            flag = br[c, src]
            hyst[c, dst] = jnp.where(flag == 1, y, jnp.where(flag == 2, -y, hf[c, src] * y))


def building_kernel(*refs):
    top, bot, u1, ret, hots, kmod, cnt, d_in, v_in, h_in, wk, st, yd, gn = refs[:14]
    now, before, d_out, v_out, h_out, ground, bufs, sem, field_sem = refs[14:]
    copies = []
    for n, (src, dst) in enumerate(
        (
            (top, now.at[pl.ds(0, 3), pl.ds(0, 8)]),
            (bot, now.at[pl.ds(0, 3), pl.ds(8, 8)]),
            (u1.at[pl.ds(0, 3), pl.ds(4, 16), pl.ds(8, 32)], before),
        )
    ):
        cp = pltpu.make_async_copy(src, dst, field_sem.at[n])
        cp.start()
        copies.append(cp)
    turned = ret[...].reshape(512, 128).T
    high = turned.astype(BF16)
    low = (turned - high.astype(F32)).astype(BF16)
    both = jnp.dot(jnp.concatenate([high, low], axis=0), hots[...], preferred_element_type=F32)
    gathered = both[:128] + both[128:]
    for j in range(8):
        g = gathered[:, 128 * j : 128 * j + 128]
        km = kmod[j : j + 1, :]
        acc = jnp.zeros((32, 128), F32)
        for k in range(4):
            acc = acc + jnp.where(km == k, g[32 * k : 32 * k + 32], 0.0)
        ground[:, 128 * j : 128 * j + 128] = acc
    outs = (d_out, v_out, h_out)
    eight = range(8)
    for c in range(3):

        def chunk(j, c=c):
            lanes = pl.ds(pl.multiple_of(j * BW, BW), BW)
            row = lax.broadcasted_iota(jnp.int32, (8, BW), 0)
            first_row = row == 0
            last_row = row == 7
            count = cnt[0:1, lanes]
            part = [pl.ds(8 * v, 8) for v in eight]

            def drift_of(x):
                below = jnp.where(first_row, 0.0, pltpu.roll(x[7], 1, 0))
                return [x[0] - below] + [x[v] - x[v - 1] for v in range(1, 8)]

            mask = [jnp.where(row * 8 + v < count, 1.0, 0.0) for v in eight]
            disp = [d_in[c, part[v], lanes] for v in eight]
            vel = [v_in[c, part[v], lanes] for v in eight]
            hyst = [h_in[c, part[v], lanes] for v in eight]
            drift = drift_of(disp)
            for t in range(STEPS):
                spring = [wk[part[v], lanes] * drift[v] + st[part[v], lanes] * hyst[v] for v in eight]
                above = spring[1:] + [jnp.where(last_row, 0.0, pltpu.roll(spring[0], 7, 0))]
                quake = ground[3 * t + c : 3 * t + c + 1, lanes]
                for v in eight:
                    push = gn[part[v], lanes] * (above[v] - spring[v]) - mask[v] * quake
                    vel[v] = vel[v] * (1.0 - DT * DAMP) + push
                    disp[v] = disp[v] + vel[v]
                new = drift_of(disp)
                for v in eight:
                    y = yd[part[v], lanes]
                    hyst[v] = jnp.minimum(jnp.maximum(hyst[v] + (new[v] - drift[v]), -y), y)
                drift = new
            for v in eight:
                dst = pl.ds(v, 8, stride=8)
                speed = vel[v] * (1.0 / DT)
                for h in range(BW // 128):
                    cut = slice(128 * h, 128 * h + 128)
                    bufs[0, c, j * (BW // 128) + h, dst] = disp[v][:, cut]
                    bufs[1, c, j * (BW // 128) + h, dst] = speed[:, cut]
                    bufs[2, c, j * (BW // 128) + h, dst] = hyst[v][:, cut]

        for_x(1024 // BW, chunk)
        for n in range(3):
            for j in range(8):
                dst = outs[n].at[c, pl.ds(0, 64), pl.ds(128 * j, 128)]
                cp = pltpu.make_async_copy(bufs.at[n, c, j], dst, sem.at[24 * c + 8 * n + j])
                cp.start()
                copies.append(cp)
    for cp in copies:
        cp.wait()


def building_start(sd, sv, hf, br, st, ms, yd, cnt):
    lanes3 = pl.BlockSpec((3, 64, 128), lambda i: (0, 0, i))
    lanes2 = pl.BlockSpec((64, 128), lambda i: (0, i))
    rows = pl.BlockSpec((1, 1, 128), lambda i: (i, 0, 0))
    return pl.pallas_call(
        building_start_kernel,
        out_shape=[sds(3, 64, 1024)] * 3 + [sds(64, 1024)] * 4,
        grid=(8,),
        in_specs=[lanes3] * 4 + [lanes2] * 3 + [rows],
        out_specs=[lanes3] * 3 + [lanes2] * 4,
        compiler_params=CP,
        name="building_start",
    )(sd, sv, hf, br, st, ms, yd, cnt.reshape(8, 1, 128))


def local(u, p, de, mu, la, sd, sv, hf, br, st, ms, yd, cnt, tile, cell):
    ix = lax.axis_index("gx")
    iy = lax.axis_index("gy")
    nx = lax.axis_size("gx")
    ny = lax.axis_size("gy")
    edge = jnp.stack([ix > 0, ix < nx - 1, iy > 0, iy < ny - 1]).astype(F32).reshape(1, 4)

    half = sds(3, 8, 32, 128)
    side = sds(3, 16, 8, 128)
    band = pltpu.VMEM((256, 128), BF16)
    work = [sds(3, 32, YR, 128), sds(6, 28, YR, 128), sds(6, 20, YR, 128), sds(16, 48, 128), sds(3, 24, YR, 128), half, half, sds(512, 128)]
    mats = [sds(3, 24, YR, 128), sds(28, YR, 128), sds(28, YR, 128), sds(24, YR, 128)]
    hbm = [pltpu.with_memory_space_constraint(x, pltpu.HBM) for x in (u, p, la, mu, de)]
    up, down, right, left = pl.pallas_call(
        pack_first_kernel,
        out_shape=[sds(XPLANES, 32, 128)] * 2 + [sds(144, 8, 128)] * 2,
        in_specs=[HB] * 5,
        out_specs=[VM] * 4,
        scratch_shapes=[pltpu.SemaphoreType.DMA((36,))],
        compiler_params=CP,
        name="pack_first",
    )(*hbm)
    north, south = ring(up, "gx", 1), ring(down, "gx", -1)
    west, east = ring(right, "gy", 1), ring(left, "gy", -1)

    req, key, kmod = pl.pallas_call(
        request_kernel,
        out_shape=[sds(128, 4, 128), sds(8, 128), sds(8, 128)],
        in_specs=[VM] * 2,
        out_specs=[VM] * 3,
        scratch_shapes=[pltpu.VMEM((512, 1024), BF16)] + [pltpu.VMEM((128, 1024), BF16)] * 2,
        compiler_params=CP,
        name="requests",
    )(tile.reshape(8, 128).astype(F32), cell.reshape(8, 128).astype(F32))
    incoming = lax.all_to_all(req, ("gx", "gy"), 0, 0, tiled=True)
    north, south, west, east, incoming = lax.optimization_barrier((north, south, west, east, incoming))

    def corners(north, south):
        n = north.shape[0]
        right, left = pl.pallas_call(
            pack_corner_kernel,
            out_shape=[sds(2, n, 8, 128)] * 2,
            in_specs=[VM] * 2,
            out_specs=[VM] * 2,
            compiler_params=CP,
            name="pack_corner",
        )(north, south)
        return ring(right, "gy", 1), ring(left, "gy", -1)

    wc, ec = corners(north, south)
    state = pl.pallas_call(
        first_round_kernel,
        out_shape=work + mats,
        in_specs=[SM] + [HB] * 5 + [VM] * 4,
        out_specs=[VM] * 12,
        scratch_shapes=[band, pltpu.SemaphoreType.DMA((9,))],
        compiler_params=CP,
        name="wave_first",
    )(edge, *hbm, north, south, west, east)
    state = pl.pallas_call(
        first_patch_kernel,
        out_shape=work + mats + [side, side],
        in_specs=[SM] + [VM] * 14,
        out_specs=[VM] * 14,
        input_output_aliases={3 + n: n for n in range(12)},
        scratch_shapes=[band],
        compiler_params=CP,
        name="patch_first",
    )(edge, wc, ec, *state)
    prev, top, bot, hist = state[4:8]
    lam, mu2, q = state[9:12]
    right, left = state[12:14]
    hists = [hist]
    for r in range(1, 4):
        north, south = ring(bot.reshape(24, 32, 128), "gx", 1), ring(top.reshape(24, 32, 128), "gx", -1)
        west, east = ring(right, "gy", 1), ring(left, "gy", -1)
        if r == 1:
            starts = building_start(sd, sv, hf, br, st, ms, yd, cnt)
            hot = pl.pallas_call(
                hot_kernel,
                out_shape=jax.ShapeDtypeStruct((4, 512, 512), BF16),
                in_specs=[VM],
                out_specs=VM,
                compiler_params=CP,
                name="hot",
            )(incoming)
            north, south, hot, starts = lax.optimization_barrier((north, south, hot, starts))
        if r == 3:
            early, hots = pl.pallas_call(
                early_answer_kernel,
                out_shape=[sds(512, 128), jax.ShapeDtypeStruct((512, 1024), BF16)],
                in_specs=[VM] * 5,
                out_specs=[VM] * 2,
                compiler_params=CP,
                name="early_answers",
            )(hot, *hists, key)
            north, south, early, hots = lax.optimization_barrier((north, south, early, hots))
        wc, ec = corners(north, south)
        consts = (prev, lam, mu2, q)
        state = pl.pallas_call(
            round_kernel,
            out_shape=work,
            in_specs=[SM] + [VM] * 10,
            out_specs=[VM] * 8,
            scratch_shapes=[band],
            compiler_params=CP,
            name="wave_round",
        )(edge, top, bot, north, south, west, east, *consts)
        state = pl.pallas_call(
            patch_kernel,
            out_shape=work + [side, side],
            in_specs=[SM] + [VM] * 14,
            out_specs=[VM] * 10,
            input_output_aliases={7 + n: n for n in range(8)},
            scratch_shapes=[band],
            compiler_params=CP,
            name="patch_round",
        )(edge, wc, ec, *consts, *state)
        prev, top, bot, hist, right, left = state[4:10]
        hists.append(hist)

    answers = pl.pallas_call(
        answer_kernel,
        out_shape=sds(128, 4, 128),
        in_specs=[VM] * 3,
        out_specs=VM,
        compiler_params=CP,
        name="answers",
    )(hot, early, hists[3])
    returned = lax.all_to_all(answers, ("gx", "gy"), 0, 0, tiled=True)
    now, before, disp, vel, hyst = pl.pallas_call(
        building_kernel,
        out_shape=[sds(3, 16, 32, 128)] * 2 + [sds(3, 64, 1024)] * 3,
        in_specs=[VM] * 14,
        out_specs=[HB] * 5,
        scratch_shapes=[
            pltpu.VMEM((32, 1024), F32),
            pltpu.VMEM((3, 3, 8, 64, 128), F32),
            pltpu.SemaphoreType.DMA((72,)),
            pltpu.SemaphoreType.DMA((3,)),
        ],
        compiler_params=CP,
        name="buildings",
    )(top, bot, prev, returned, hots, kmod, cnt.reshape(1, 1024), *starts)
    return now, before, disp, vel, hyst


def solution(mesh):
    grid = P(None, "gx", "gy", None)
    cells = P("gx", "gy", None)
    both = ("gx", "gy")
    b3 = P(None, None, both)
    b2 = P(None, both)
    b1 = P(both)
    return jax.shard_map(
        local,
        mesh=mesh,
        in_specs=(grid, grid, cells, cells, cells, b3, b3, b3, b3, b2, b2, b2, b1, P(both, None), b1),
        out_specs=(grid, grid, b3, b3, b3),
        check_vma=False,
    )
```

```python
import jax
import jax.numpy as jnp
from jax import lax
from jax.experimental import pallas as pl
from jax.experimental.pallas import tpu as pltpu
from jax.sharding import PartitionSpec as P

STEPS = 8
DT = 0.35
POST = 0.1
DAMP = 0.05
F32 = jnp.float32
BF16 = jnp.bfloat16
VM = pl.BlockSpec(memory_space=pltpu.VMEM)
SM = pl.BlockSpec(memory_space=pltpu.SMEM)
HB = pl.BlockSpec(memory_space=pltpu.HBM)
CP = pltpu.CompilerParams(vmem_limit_bytes=12 << 20)
BW = 128
YR = 56

XPARTS = ((0, 3, 8), (1, 3, 4), (2, 1, 6), (3, 1, 6), (4, 1, 4))
XPLANES = sum(c * w for _, c, w in XPARTS)


def sds(*shape):
    return jax.ShapeDtypeStruct(shape, F32)


def ring(x, axis, step):
    n = lax.axis_size(axis)
    return lax.ppermute(x, axis, [(i, (i + step) % n) for i in range(n)])


def split3(x):
    hi = x.astype(BF16)
    rest = x - hi.astype(F32)
    mid = rest.astype(BF16)
    low = (rest - mid.astype(F32)).astype(BF16)
    return hi, mid, low


def at_comp(ref, comps, c, rows, cols):
    return ref.at[c, rows, cols] if comps == 3 else ref.at[rows, cols]


def pack_first_kernel(u, p, la, mu, de, up, down, right, left, sem):
    args = (u, p, la, mu, de)
    copies = []
    off = 0
    row = 0
    for a, comps, w in XPARTS:
        for c in range(comps):
            full = pl.ds(0, 32)
            every = pl.ds(0, 16)
            for src, dst in (
                (at_comp(args[a], comps, c, pl.ds(16 - w, w), full), up.at[pl.ds(off, w)]),
                (at_comp(args[a], comps, c, pl.ds(0, w), full), down.at[pl.ds(off, w)]),
                (at_comp(args[a], comps, c, every, pl.ds(24, 8)), right.at[pl.ds(row, 16)]),
                (at_comp(args[a], comps, c, every, pl.ds(0, 8)), left.at[pl.ds(row, 16)]),
            ):
                cp = pltpu.make_async_copy(src, dst, sem.at[len(copies)])
                cp.start()
                copies.append(cp)
            off += w
            row += 16
    for cp in copies:
        cp.wait()


def pack_corner_kernel(north, south, right, left):
    for dst, col in ((right, 24), (left, 0)):
        dst[0] = north[:, col : col + 8]
        dst[1] = south[:, col : col + 8]


def z_matrix():
    i = lax.broadcasted_iota(jnp.int32, (256, 128), 0)
    j = lax.broadcasted_iota(jnp.int32, (256, 128), 1)
    d = jnp.where(i < 128, i, i - 128) - j
    one = jnp.ones((256, 128), F32)
    near = jnp.where(d == 1, 8.0 * one, 0.0) - jnp.where(d == -1, 8.0 * one, 0.0)
    far = jnp.where(d == 2, one, 0.0) - jnp.where(d == -2, one, 0.0)
    return (near - far).astype(BF16)


def pieces2(f):
    hi = f.astype(BF16)
    lo = (f - hi.astype(F32)).astype(BF16)
    return jnp.concatenate([hi, lo], axis=1)


def dz_all(fields, mz):
    n = fields[0].shape[0]
    lhs = pieces2(jnp.concatenate(fields, axis=0))
    out = jnp.dot(lhs, mz, preferred_element_type=F32)
    return [out[n * k : n * k + n] for k in range(len(fields))]


def dx(rows, k):
    return 8.0 * (rows[k + 3] - rows[k + 1]) - (rows[k + 4] - rows[k])


def dy(ref, c, x, y, n):
    near = ref[c, x, pl.ds(y + 1, n)] - ref[c, x, pl.ds(y - 1, n)]
    far = ref[c, x, pl.ds(y + 2, n)] - ref[c, x, pl.ds(y - 2, n)]
    return 8.0 * near - far


def for_x(count, fn):
    def body(i, carry):
        fn(i)
        return carry

    lax.fori_loop(0, count, body, 0)


def stress_rows(u, ux, s, sx, lam, mu, mz, blocks, m, n):
    rows = []
    fields = []
    for g0, y in blocks:
        r = [[u[c, g0 - ux - 2 + j, pl.ds(y, n)] for j in range(m + 4)] for c in range(3)]
        rows.append(r)
        fields += [r[c][k + 2] for k in range(m) for c in range(3)]
    zs = dz_all(fields, mz[...])
    for (g0, y), r in zip(blocks, rows):
        ys = pl.ds(y, n)
        for k in range(m):
            gx = g0 + k
            x = gx - ux
            z0, z1, z2 = zs[:3]
            zs = zs[3:]
            mm = mu[gx - 2, ys]
            g00 = dx(r[0], k)
            g11 = dy(u, 1, x, y, n)
            lt = lam[gx - 2, ys] * (g00 + g11 + z2)
            m2 = mm + mm
            s[0, gx - sx, ys] = lt + m2 * g00
            s[1, gx - sx, ys] = lt + m2 * g11
            s[2, gx - sx, ys] = lt + m2 * z2
            s[3, gx - sx, ys] = mm * (dy(u, 0, x, y, n) + dx(r[1], k))
            s[4, gx - sx, ys] = mm * (z0 + dx(r[2], k))
            s[5, gx - sx, ys] = mm * (z1 + dy(u, 2, x, y, n))


def forces(s, sx, q, mz, blocks, m, n):
    rows = []
    fields = []
    for g0, y in blocks:
        ys = pl.ds(y, n)
        r = [[s[c, g0 - sx - 2 + j, ys] for j in range(m + 4)] for c in (0, 3, 4)]
        rows.append(r)
        for k in range(m):
            fields += [r[2][k + 2], s[5, g0 - sx + k, ys], s[2, g0 - sx + k, ys]]
    zs = dz_all(fields, mz[...])
    out = []
    for (g0, y), r in zip(blocks, rows):
        mine = []
        for k in range(m):
            x = g0 + k
            z0, z1, z2 = zs[:3]
            zs = zs[3:]
            qk = q[x - 4, pl.ds(y, n)]
            mine.append(
                (
                    qk * (dx(r[0], k) + dy(s, 3, x - sx, y, n) + z0),
                    qk * (dx(r[1], k) + dy(s, 1, x - sx, y, n) + z1),
                    qk * (dx(r[2], k) + dy(s, 5, x - sx, y, n) + z2),
                )
            )
        out.append(mine)
    return out


def surface(fs, slot, old):
    lane = lax.broadcasted_iota(jnp.int32, fs[0].shape, 1)
    for c, f in enumerate(fs):
        v = pltpu.roll(f, slot + c, 1) if slot + c else f
        old = jnp.where(lane == slot + c, v, old)
    return old


def first_rows(ue, prev, q, s, hs, mz, u1, blocks, m, n, seen):
    for (i0, y), fr in zip(blocks, forces(s, 2, q, mz, [(i0 + 4, y) for i0, y in blocks], m, n)):
        ys = pl.ds(y, n)
        for k, fs in enumerate(fr):
            i = i0 + k
            if k in seen(i0):
                hs[i - 4, pl.ds(y - 4, n)] = surface(fs, 0, jnp.zeros((n, 128), F32))
            for c in range(3):
                now = ue[c, i + 4, ys]
                u1[c, i, ys] = (now - prev[c, i, ys]) + (now + fs[c])


def second_rows(ue, q, s, hs, mz, u1, hist, blocks, m, n):
    places = [(j0 + 8 * part + 8, y) for _, j0, part, y, _ in blocks]
    for (out, j0, part, y, side), fr in zip(blocks, forces(s, 6, q, mz, places, m, n)):
        ys = pl.ds(y, n)
        for k, fs in enumerate(fr):
            i = j0 + 8 * part + k
            r = i * 32 + y - 8
            hist[pl.ds(r, n)] = surface(fs, 3, hs[i, pl.ds(y - 4, n)])
            for c in range(3):
                now = u1[c, i + 4, ys]
                v = (now - ue[c, i + 8, ys]) + (now + fs[c])
                out[c, j0 + k, pl.ds(y - 8, n)] = v
                if side is not None:
                    side[c, i] = v


def two_steps(prev, lam, mu, q, ue, s, s2, hs, u1, top, bot, hist, mz):
    mz[...] = z_matrix()
    none = lambda i0: ()
    every = lambda i0: range(8)
    for_x(2, lambda i: stress_rows(ue, 0, s, 2, lam, mu, mz, [(14 * i + 2, 2)], 14, 48))
    first_rows(ue, prev, q, s, hs, mz, u1, [(0, 4), (20, 4)], 4, 48, none)
    for_x(2, lambda i: first_rows(ue, prev, q, s, hs, mz, u1, [(8 * i + 4, 4)], 8, 48, every))
    for_x(2, lambda i: stress_rows(u1, 4, s2, 6, lam, mu, mz, [(10 * i + 6, 6)], 10, 48))
    for part, out in enumerate((top, bot)):
        second_rows(ue, q, s2, hs, mz, u1, hist, [(out, 0, part, 8, None)], 8, 32)


def patch_two_steps(prev, lam, mu, q, ue, s, s2, hs, u1, top, bot, hist, right, left, mz):
    mz[...] = z_matrix()
    stress_rows(ue, 0, s, 2, lam, mu, mz, [(x, y) for x in (2, 22) for y in (2, 38)], 8, 8)
    seen = lambda i0: range(4, 8) if i0 == 0 else range(4)
    first_rows(ue, prev, q, s, hs, mz, u1, [(i, y) for i in (0, 16) for y in (4, 36)], 8, 8, seen)
    stress_rows(u1, 4, s2, 6, lam, mu, mz, [(x, y) for x in (6, 18) for y in (6, 34)], 8, 8)
    blocks = [(o, 0, part, y, side) for part, o in enumerate((top, bot)) for y, side in ((8, left), (32, right))]
    second_rows(ue, q, s2, hs, mz, u1, hist, blocks, 8, 8)


def first_round_kernel(flags, u, p, la, mu, de, north, south, west, east, ue, s, s2, hs, u1, top, bot, hist, pe, lam, muo, q, mz, sem):
    fn, fs, fw, fe = [flags[0, k] for k in range(4)]
    copies = []
    args = (u, p, la, mu, de)
    exts = (ue, pe, lam, muo, q)
    off = 0
    row = 0
    for a, comps, w in XPARTS:
        for c in range(comps):
            ref = exts[a].at[c] if comps == 3 else exts[a]
            arg = args[a].at[c] if comps == 3 else args[a]
            cp = pltpu.make_async_copy(arg, ref.at[pl.ds(w, 16), pl.ds(8, 32)], sem.at[len(copies)])
            cp.start()
            copies.append(cp)
            none = jnp.zeros((w, 8, 128), F32)
            for x, strip, f in ((0, north, fn), (16 + w, south, fs)):
                ref[x : x + w, 0:8] = none
                ref[x : x + w, 8:40] = strip[off : off + w] * f
                ref[x : x + w, 40:48] = none
            ref[w : w + 16, 0:8] = west[row : row + 16] * fw
            ref[w : w + 16, 40:48] = east[row : row + 16] * fe
            off += w
            row += 16
    for cp in copies:
        cp.wait()

    lam[:, 0:48] = lam[:, 0:48] * (1.0 / 12.0)
    muo[:, 0:48] = muo[:, 0:48] * (1.0 / 12.0)
    q[:, 0:48] = inverse_density(q[:, 0:48])
    two_steps(pe, lam, muo, q, ue, s, s2, hs, u1, top, bot, hist, mz)


def inverse_density(d):
    return jnp.where(d > 0.0, (DT * DT / 12.0) / jnp.where(d > 0.0, d, 1.0), 0.0)


def first_patch_kernel(*refs):
    flags, wc, ec = refs[:3]
    ue, s, s2, hs, u1, top, bot, hist, pe, lam, mu, q, right, left, mz = refs[15:]
    fn, fs, fw, fe = [flags[0, k] for k in range(4)]
    exts = (ue, pe, lam, mu, q)
    off = 0
    for a, comps, w in XPARTS:
        for c in range(comps):
            ref = exts[a].at[c] if comps == 3 else exts[a]
            for half, x, f in ((0, 0, fn), (1, 16 + w, fs)):
                for strip, y, g in ((wc, 0, fw), (ec, 40, fe)):
                    v = strip[half, off : off + w] * (f * g)
                    if a in (2, 3):
                        v = v * (1.0 / 12.0)
                    ref[x : x + w, y : y + 8] = inverse_density(v) if a == 4 else v
            off += w
    patch_two_steps(pe, lam, mu, q, ue, s, s2, hs, u1, top, bot, hist, right, left, mz)


def round_kernel(flags, top, bot, north, south, west, east, prev, lam, mu, q, ue, s, s2, hs, u1, top2, bot2, hist, mz):
    fn, fs, fw, fe = [flags[0, k] for k in range(4)]
    none = jnp.zeros((8, 8, 128), F32)
    for c in range(3):
        for x, strip, f in ((0, north, fn), (24, south, fs)):
            ue[c, x : x + 8, 0:8] = none
            ue[c, x : x + 8, 8:40] = strip[8 * c : 8 * c + 8] * f
            ue[c, x : x + 8, 40:48] = none
        ue[c, 8:24, 0:8] = west[c] * fw
        ue[c, 8:16, 8:40] = top[c]
        ue[c, 16:24, 8:40] = bot[c]
        ue[c, 8:24, 40:48] = east[c] * fe
    two_steps(prev, lam, mu, q, ue, s, s2, hs, u1, top2, bot2, hist, mz)


def fill_corners(flags, wc, ec, ue):
    fn, fs, fw, fe = [flags[0, k] for k in range(4)]
    for c in range(3):
        for half, x, f in ((0, 0, fn), (1, 24, fs)):
            ue[c, x : x + 8, 0:8] = wc[half, 8 * c : 8 * c + 8] * (f * fw)
            ue[c, x : x + 8, 40:48] = ec[half, 8 * c : 8 * c + 8] * (f * fe)


def patch_kernel(*refs):
    flags, wc, ec, prev, lam, mu, q = refs[:7]
    ue, s, s2, hs, u1, top, bot, hist, right, left, mz = refs[15:]
    fill_corners(flags, wc, ec, ue)
    patch_two_steps(prev, lam, mu, q, ue, s, s2, hs, u1, top, bot, hist, right, left, mz)


def request_kernel(tiles, cells, req, key, kmod, a_ref, bhi, blo, near, sem):
    copies = [pltpu.make_async_copy(src, near.at[n], sem.at[n]) for n, src in enumerate((tiles, cells))]
    for cp in copies:
        cp.start()
    for cp in copies:
        cp.wait()
    tile = near[0].astype(F32)
    cell = near[1].astype(F32)
    ones = jnp.ones((128, 128), F32)
    sub = lax.broadcasted_iota(jnp.int32, (128, 128), 0)
    lan = lax.broadcasted_iota(jnp.int32, (128, 128), 1)
    cols = [(ones * tile[i : i + 1, :]).T for i in range(8)]
    row512 = lax.broadcasted_iota(jnp.int32, (512, 128), 0).astype(F32)
    subf = sub.astype(F32)
    for j in range(8):
        mine = tile[j : j + 1, :]
        acc = jnp.where((cols[j] == mine) & (sub < lan), 1.0, 0.0)
        for i in range(j):
            acc = acc + jnp.where(cols[i] == mine, 1.0, 0.0)
        rank = jnp.sum(acc, axis=0, keepdims=True)
        quarter = jnp.floor(rank * 0.25)
        kj = mine * 4.0 + quarter
        mj = rank - 4.0 * quarter
        key[j : j + 1, :] = kj
        kmod[j : j + 1, :] = mj
        lanes = pl.ds(128 * j, 128)
        a_ref[:, lanes] = jnp.where(row512 == kj, 1.0, 0.0).astype(BF16)
        cj = cell[j : j + 1, :]
        hi = jnp.floor(cj * (1.0 / 32.0))
        hit = subf == mj
        bhi[:, lanes] = jnp.where(hit, hi, 0.0).astype(BF16)
        blo[:, lanes] = jnp.where(hit, cj - 32.0 * hi, 0.0).astype(BF16)
    dims = (((1,), (1,)), ((), ()))
    top = lax.dot_general(a_ref[...], bhi[...], dims, preferred_element_type=F32)
    low = lax.dot_general(a_ref[...], blo[...], dims, preferred_element_type=F32)
    req[...] = (32.0 * top + low).reshape(128, 4, 128)


def hot_kernel(inc, hot):
    cells = inc[...].reshape(512, 128)
    lane = lax.broadcasted_iota(jnp.int32, (512, 512), 1).astype(F32)
    for k in range(4):
        hot[k] = jnp.where(lane == cells[:, k : k + 1], 1.0, 0.0).astype(BF16)


def pick(h, hot):
    acc = jnp.zeros((512, 128), F32)
    for k in range(4):
        hk = pltpu.roll(h, 32 * k, 1) if k else h
        hi = hk.astype(BF16)
        mid = (hk - hi.astype(F32)).astype(BF16)
        both = jnp.dot(hot[k], jnp.concatenate([hi, mid], axis=1), preferred_element_type=F32)
        acc = acc + (both[:, :128] + both[:, 128:])
    return acc


def early_answer_kernel(hot, h0, h1, h2, key, out, hots):
    row512 = lax.broadcasted_iota(jnp.int32, (512, 128), 0).astype(F32)
    for j in range(8):
        hots[:, 128 * j : 128 * j + 128] = jnp.where(row512 == key[j : j + 1, :], 1.0, 0.0).astype(BF16)
    h = h0[...] + pltpu.roll(h1[...], 6, 1) + pltpu.roll(h2[...], 12, 1)
    out[...] = pick(h, hot)


def answer_kernel(hot, early, h3, out):
    out[...] = (early[...] + pick(pltpu.roll(h3[...], 18, 1), hot)).reshape(128, 4, 128)


def building_start_kernel(d_in, v_in, hf, br, st, ms, yd, cnt, disp, vel, hyst, weak, stiff, yld, gain):
    low = lax.broadcasted_iota(jnp.int32, (8, 128), 0) * 8
    for v in range(8):
        src = pl.ds(v, 8, stride=8)
        dst = pl.ds(8 * v, 8)
        mask = jnp.where(low + v < cnt[0], 1.0, 0.0)
        y = yd[src] * mask
        k = st[src] * mask
        weak[dst] = POST * k
        stiff[dst] = (1.0 - POST) * k
        yld[dst] = y
        gain[dst] = DT * DT / ms[src]
        for c in range(3):
            disp[c, dst] = d_in[c, src] * mask
            vel[c, dst] = v_in[c, src] * (DT * mask)
            flag = br[c, src]
            hyst[c, dst] = jnp.where(flag == 1, y, jnp.where(flag == 2, -y, hf[c, src] * y))


def building_kernel(*refs):
    top, bot, u1, ret, hots, kmod, cnt, d_in, v_in, h_in, wk, st, yd, gn = refs[:14]
    now, before, d_out, v_out, h_out, ground, bufs, sem, field_sem = refs[14:]
    copies = []
    for n, (src, dst) in enumerate(
        (
            (top, now.at[pl.ds(0, 3), pl.ds(0, 8)]),
            (bot, now.at[pl.ds(0, 3), pl.ds(8, 8)]),
            (u1.at[pl.ds(0, 3), pl.ds(4, 16), pl.ds(8, 32)], before),
        )
    ):
        cp = pltpu.make_async_copy(src, dst, field_sem.at[n])
        cp.start()
        copies.append(cp)
    turned = ret[...].reshape(512, 128).T
    high = turned.astype(BF16)
    low = (turned - high.astype(F32)).astype(BF16)
    both = jnp.dot(jnp.concatenate([high, low], axis=0), hots[...], preferred_element_type=F32)
    gathered = both[:128] + both[128:]
    for j in range(8):
        g = gathered[:, 128 * j : 128 * j + 128]
        km = kmod[j : j + 1, :]
        acc = jnp.zeros((32, 128), F32)
        for k in range(4):
            acc = acc + jnp.where(km == k, g[32 * k : 32 * k + 32], 0.0)
        ground[:, 128 * j : 128 * j + 128] = acc
    outs = (d_out, v_out, h_out)
    eight = range(8)
    for c in range(3):

        def chunk(j, c=c):
            lanes = pl.ds(pl.multiple_of(j * BW, BW), BW)
            row = lax.broadcasted_iota(jnp.int32, (8, BW), 0)
            first_row = row == 0
            last_row = row == 7
            count = cnt[0:1, lanes]
            part = [pl.ds(8 * v, 8) for v in eight]

            def drift_of(x):
                below = jnp.where(first_row, 0.0, pltpu.roll(x[7], 1, 0))
                return [x[0] - below] + [x[v] - x[v - 1] for v in range(1, 8)]

            mask = [jnp.where(row * 8 + v < count, 1.0, 0.0) for v in eight]
            disp = [d_in[c, part[v], lanes] for v in eight]
            vel = [v_in[c, part[v], lanes] for v in eight]
            hyst = [h_in[c, part[v], lanes] for v in eight]
            drift = drift_of(disp)
            for t in range(STEPS):
                spring = [wk[part[v], lanes] * drift[v] + st[part[v], lanes] * hyst[v] for v in eight]
                above = spring[1:] + [jnp.where(last_row, 0.0, pltpu.roll(spring[0], 7, 0))]
                quake = ground[3 * t + c : 3 * t + c + 1, lanes]
                for v in eight:
                    push = gn[part[v], lanes] * (above[v] - spring[v]) - mask[v] * quake
                    vel[v] = vel[v] * (1.0 - DT * DAMP) + push
                    disp[v] = disp[v] + vel[v]
                new = drift_of(disp)
                for v in eight:
                    y = yd[part[v], lanes]
                    hyst[v] = jnp.minimum(jnp.maximum(hyst[v] + (new[v] - drift[v]), -y), y)
                drift = new
            for v in eight:
                dst = pl.ds(v, 8, stride=8)
                speed = vel[v] * (1.0 / DT)
                for h in range(BW // 128):
                    cut = slice(128 * h, 128 * h + 128)
                    bufs[0, c, j * (BW // 128) + h, dst] = disp[v][:, cut]
                    bufs[1, c, j * (BW // 128) + h, dst] = speed[:, cut]
                    bufs[2, c, j * (BW // 128) + h, dst] = hyst[v][:, cut]

        for_x(1024 // BW, chunk)
        for n in range(3):
            for j in range(8):
                dst = outs[n].at[c, pl.ds(0, 64), pl.ds(128 * j, 128)]
                cp = pltpu.make_async_copy(bufs.at[n, c, j], dst, sem.at[24 * c + 8 * n + j])
                cp.start()
                copies.append(cp)
    for cp in copies:
        cp.wait()


def building_start(sd, sv, hf, br, st, ms, yd, cnt):
    lanes3 = pl.BlockSpec((3, 64, 128), lambda i: (0, 0, i))
    lanes2 = pl.BlockSpec((64, 128), lambda i: (0, i))
    rows = pl.BlockSpec((1, 1, 128), lambda i: (i, 0, 0))
    return pl.pallas_call(
        building_start_kernel,
        out_shape=[sds(3, 64, 1024)] * 3 + [sds(64, 1024)] * 4,
        grid=(8,),
        in_specs=[lanes3] * 4 + [lanes2] * 3 + [rows],
        out_specs=[lanes3] * 3 + [lanes2] * 4,
        compiler_params=CP,
        name="building_start",
    )(sd, sv, hf, br, st, ms, yd, cnt.reshape(8, 1, 128))


def local(u, p, de, mu, la, sd, sv, hf, br, st, ms, yd, cnt, tile, cell):
    ix = lax.axis_index("gx")
    iy = lax.axis_index("gy")
    nx = lax.axis_size("gx")
    ny = lax.axis_size("gy")
    edge = jnp.stack([ix > 0, ix < nx - 1, iy > 0, iy < ny - 1]).astype(F32).reshape(1, 4)

    half = sds(3, 8, 32, 128)
    side = sds(3, 16, 8, 128)
    band = pltpu.VMEM((256, 128), BF16)
    work = [sds(3, 32, YR, 128), sds(6, 28, YR, 128), sds(6, 20, YR, 128), sds(16, 48, 128), sds(3, 24, YR, 128), half, half, sds(512, 128)]
    mats = [sds(3, 24, YR, 128), sds(28, YR, 128), sds(28, YR, 128), sds(24, YR, 128)]
    hbm = [pltpu.with_memory_space_constraint(x, pltpu.HBM) for x in (u, p, la, mu, de)]
    up, down, right, left = pl.pallas_call(
        pack_first_kernel,
        out_shape=[sds(XPLANES, 32, 128)] * 2 + [sds(144, 8, 128)] * 2,
        in_specs=[HB] * 5,
        out_specs=[VM] * 4,
        scratch_shapes=[pltpu.SemaphoreType.DMA((36,))],
        compiler_params=CP,
        name="pack_first",
    )(*hbm)
    north, south = ring(up, "gx", 1), ring(down, "gx", -1)
    west, east = ring(right, "gy", 1), ring(left, "gy", -1)

    req, key, kmod = pl.pallas_call(
        request_kernel,
        out_shape=[sds(128, 4, 128), sds(8, 128), sds(8, 128)],
        in_specs=[HB] * 2,
        out_specs=[VM] * 3,
        scratch_shapes=[pltpu.VMEM((512, 1024), BF16)] + [pltpu.VMEM((128, 1024), BF16)] * 2
        + [pltpu.VMEM((2, 8, 128), jnp.int32), pltpu.SemaphoreType.DMA((2,))],
        compiler_params=CP,
        name="requests",
    )(*[pltpu.with_memory_space_constraint(x.reshape(8, 128), pltpu.HBM) for x in (tile, cell)])
    incoming = lax.all_to_all(req, ("gx", "gy"), 0, 0, tiled=True)
    north, south, west, east, incoming = lax.optimization_barrier((north, south, west, east, incoming))

    def corners(north, south):
        n = north.shape[0]
        right, left = pl.pallas_call(
            pack_corner_kernel,
            out_shape=[sds(2, n, 8, 128)] * 2,
            in_specs=[VM] * 2,
            out_specs=[VM] * 2,
            compiler_params=CP,
            name="pack_corner",
        )(north, south)
        return ring(right, "gy", 1), ring(left, "gy", -1)

    wc, ec = corners(north, south)
    state = pl.pallas_call(
        first_round_kernel,
        out_shape=work + mats,
        in_specs=[SM] + [HB] * 5 + [VM] * 4,
        out_specs=[VM] * 12,
        scratch_shapes=[band, pltpu.SemaphoreType.DMA((9,))],
        compiler_params=CP,
        name="wave_first",
    )(edge, *hbm, north, south, west, east)
    state = pl.pallas_call(
        first_patch_kernel,
        out_shape=work + mats + [side, side],
        in_specs=[SM] + [VM] * 14,
        out_specs=[VM] * 14,
        input_output_aliases={3 + n: n for n in range(12)},
        scratch_shapes=[band],
        compiler_params=CP,
        name="patch_first",
    )(edge, wc, ec, *state)
    prev, top, bot, hist = state[4:8]
    lam, mu2, q = state[9:12]
    right, left = state[12:14]
    hists = [hist]
    for r in range(1, 4):
        north, south = ring(bot.reshape(24, 32, 128), "gx", 1), ring(top.reshape(24, 32, 128), "gx", -1)
        west, east = ring(right, "gy", 1), ring(left, "gy", -1)
        if r == 1:
            starts = building_start(sd, sv, hf, br, st, ms, yd, cnt)
            hot = pl.pallas_call(
                hot_kernel,
                out_shape=jax.ShapeDtypeStruct((4, 512, 512), BF16),
                in_specs=[VM],
                out_specs=VM,
                compiler_params=CP,
                name="hot",
            )(incoming)
            north, south, hot, starts = lax.optimization_barrier((north, south, hot, starts))
        if r == 3:
            early, hots = pl.pallas_call(
                early_answer_kernel,
                out_shape=[sds(512, 128), jax.ShapeDtypeStruct((512, 1024), BF16)],
                in_specs=[VM] * 5,
                out_specs=[VM] * 2,
                compiler_params=CP,
                name="early_answers",
            )(hot, *hists, key)
            north, south, early, hots = lax.optimization_barrier((north, south, early, hots))
        wc, ec = corners(north, south)
        consts = (prev, lam, mu2, q)
        state = pl.pallas_call(
            round_kernel,
            out_shape=work,
            in_specs=[SM] + [VM] * 10,
            out_specs=[VM] * 8,
            scratch_shapes=[band],
            compiler_params=CP,
            name="wave_round",
        )(edge, top, bot, north, south, west, east, *consts)
        state = pl.pallas_call(
            patch_kernel,
            out_shape=work + [side, side],
            in_specs=[SM] + [VM] * 14,
            out_specs=[VM] * 10,
            input_output_aliases={7 + n: n for n in range(8)},
            scratch_shapes=[band],
            compiler_params=CP,
            name="patch_round",
        )(edge, wc, ec, *consts, *state)
        prev, top, bot, hist, right, left = state[4:10]
        hists.append(hist)

    answers = pl.pallas_call(
        answer_kernel,
        out_shape=sds(128, 4, 128),
        in_specs=[VM] * 3,
        out_specs=VM,
        compiler_params=CP,
        name="answers",
    )(hot, early, hists[3])
    returned = lax.all_to_all(answers, ("gx", "gy"), 0, 0, tiled=True)
    now, before, disp, vel, hyst = pl.pallas_call(
        building_kernel,
        out_shape=[sds(3, 16, 32, 128)] * 2 + [sds(3, 64, 1024)] * 3,
        in_specs=[VM] * 14,
        out_specs=[HB] * 5,
        scratch_shapes=[
            pltpu.VMEM((32, 1024), F32),
            pltpu.VMEM((3, 3, 8, 64, 128), F32),
            pltpu.SemaphoreType.DMA((72,)),
            pltpu.SemaphoreType.DMA((3,)),
        ],
        compiler_params=CP,
        name="buildings",
    )(top, bot, prev, returned, hots, kmod, cnt.reshape(1, 1024), *starts)
    return now, before, disp, vel, hyst


def solution(mesh):
    grid = P(None, "gx", "gy", None)
    cells = P("gx", "gy", None)
    both = ("gx", "gy")
    b3 = P(None, None, both)
    b2 = P(None, both)
    b1 = P(both)
    return jax.shard_map(
        local,
        mesh=mesh,
        in_specs=(grid, grid, cells, cells, cells, b3, b3, b3, b3, b2, b2, b2, b1, P(both, None), b1),
        out_specs=(grid, grid, b3, b3, b3),
        check_vma=False,
    )
```
